32 devices in a mesh: survey: 4 (over z), tile: 8 (over y, x, core).
Axes of the slice: x: 2, y: 2, z: 4, core: 2. Of those that a mesh axis runs over, the one named last changes fastest.
Arguments:
- data: bfloat16 [4, 64, 128, 256], P('survey', 'tile'), may hold values from -12 to 12
- correlation_index: int32 [4, 8, 4, 128], P(None, 'tile'), may hold values from 0 to 1023, as said below
- correlation_count: int32 [4, 8, 4], P(None, 'tile'), may hold values from 0 to 128, as said below
- smoothing: float32 [3], replicated, may hold values from 0.5 to 4
Outputs:
- fields: float32 [4, 3, 64, 128], P('survey', None, 'tile')
- volume: bfloat16 [4, 64, 128, 256], P('survey', 'tile')
The draws below stay inside these ranges and needn't reach their ends.
Inputs may be any that keep to these rules, and one draw needn't show every extreme that they name: `correlation_index`: each list holds 128 consecutive positions of the tile. `correlation_count`: zero where s equals p; one or more where s is p + 1 modulo 4; in every draw one tile and one destination group receive 128 live slots from every other group.
All inputs are finite; a program needn't handle non-finite values.
Results may differ from the reference program's by a relative error of at most 0.0014.
Values may be sent and summed in bfloat16 or wider, within the bound.
No kernel may reach another device: no remote copies, remote signals or barrier semaphores. Data moves between devices by JAX's collectives and lax.ppermute only.
A program may use at most 64 MiB of HBM per device.

```python
import math
import jax
import jax.numpy as jnp
from jax import lax

TX = 8
TY = 128
NT = 256
CAP = 128
ROUNDS = 2
CG_ITERS = 3
SURVEYS = 4
TILES = 8
NXTOT = 64
N_TILE = 8


def time_smooth(raw_noise):
    tap_weights = (1.0, 2.0, 3.0, 2.0, 1.0)
    smoothed = jnp.zeros_like(raw_noise)
    for offset in range(5):
        smoothed = smoothed + tap_weights[offset] * jnp.roll(raw_noise, offset - 2, axis=-1)
    return smoothed / math.sqrt(19.0)


def draw_data(key, part):
    split_keys = jax.random.split(jax.random.fold_in(key, 101), 9)
    base_key, gain_key, wobble_key, level_key, noise_key = (split_keys[0], split_keys[1], split_keys[2], split_keys[3], split_keys[4])
    whole_key, phase_key, trend_key, rough_key = (split_keys[5], split_keys[6], split_keys[7], split_keys[8])
    full_shape = (SURVEYS, NXTOT, TY, NT)
    raw_base = jax.random.normal(base_key, (1, NXTOT, TY, NT), jnp.float32)
    noise_part = jax.random.normal(noise_key, full_shape, jnp.float32)
    common = 1.5 * time_smooth(raw_base)
    delayed_list = []
    for delay_steps in range(3):
        delayed_list.append(jnp.roll(common[0], delay_steps, axis=-1))
    delayed = jnp.stack(delayed_list)
    whole_delay = jax.random.randint(whole_key, (SURVEYS,), 0, 2)
    phases = jax.random.uniform(phase_key, (4, SURVEYS, 1, 1, 1), jnp.float32, -math.pi, math.pi)
    inline_pos = jnp.arange(NXTOT, dtype=jnp.float32)[None, :, None, None] / NXTOT
    cross_pos = jnp.arange(TY, dtype=jnp.float32)[None, None, :, None] / TY
    rough_part = jax.random.uniform(rough_key, (SURVEYS, NXTOT, TY, 1), jnp.float32, -1.0, 1.0)
    fraction = 0.5 + 0.2 * jnp.sin(2.0 * math.pi * inline_pos + phases[0]) + 0.15 * jnp.sin(2.0 * math.pi * cross_pos + phases[1]) + 0.1 * rough_part
    earlier = jnp.take(delayed, whole_delay, axis=0)
    later = jnp.take(delayed, whole_delay + 1, axis=0)
    shifted = earlier + fraction * (later - earlier)
    trend = jax.random.uniform(trend_key, (SURVEYS, 1, 1, 1), jnp.float32, -0.5, 0.5) + 0.15 * jnp.sin(2.0 * math.pi * inline_pos + phases[2]) + 0.1 * jnp.sin(2.0 * math.pi * cross_pos + phases[3])
    time_pos = (jnp.arange(NT, dtype=jnp.float32) - (NT - 1) / 2.0) / (NT / 2.0)
    group_gain = jnp.exp(0.4 * jax.random.normal(gain_key, (SURVEYS, 1, 1, 1), jnp.float32))
    wobble = 1.0 + 0.3 * jax.random.uniform(wobble_key, (SURVEYS, NXTOT, TY, 1), jnp.float32, -1.0, 1.0)
    noise_level = jnp.exp(jax.random.uniform(level_key, (SURVEYS, 1, 1, 1), jnp.float32, math.log(0.15), 0.0))
    amplitude = group_gain * wobble * jnp.exp(trend * time_pos)
    values = amplitude * shifted + noise_level * noise_part
    return jnp.clip(values, -12.0, 12.0).astype(jnp.bfloat16)


def draw_correlation_count(key, part):
    draw_key, tile_key, group_key = jax.random.split(jax.random.fold_in(key, 202), 3)
    counts = jax.random.randint(draw_key, (SURVEYS, TILES, SURVEYS), 0, CAP + 1)
    source_ids = jnp.arange(SURVEYS, dtype=jnp.int32)[:, None, None]
    tile_ids = jnp.arange(TILES, dtype=jnp.int32)[None, :, None]
    dest_ids = jnp.arange(SURVEYS, dtype=jnp.int32)[None, None, :]
    busy_tile = jax.random.randint(tile_key, (), 0, TILES)
    busy_group = jax.random.randint(group_key, (), 0, SURVEYS)
    counts = jnp.where((tile_ids == busy_tile) & (dest_ids == busy_group), CAP, counts)
    neighbour = (dest_ids + 1) % SURVEYS
    counts = jnp.where(source_ids == neighbour, jnp.maximum(counts, 1), counts)
    counts = jnp.where(source_ids == dest_ids, 0, counts)
    return counts.astype(jnp.int32)


def draw_correlation_index(key, part):
    start_key, tile_key = jax.random.split(jax.random.fold_in(key, 303))
    trace_total = TX * TY
    starts = jax.random.randint(start_key, (SURVEYS, TILES, SURVEYS, 1), 0, trace_total - CAP + 1)
    edge_tile = jax.random.randint(tile_key, (), 0, TILES)
    tile_ids = jnp.arange(TILES, dtype=jnp.int32)[None, :, None, None]
    source_ids = jnp.arange(SURVEYS, dtype=jnp.int32)[:, None, None, None]
    starts = jnp.where((tile_ids == edge_tile) & (source_ids == 0), trace_total - CAP, starts)
    starts = jnp.where((tile_ids == edge_tile) & (source_ids == SURVEYS - 1), 0, starts)
    slot_ids = jnp.arange(CAP, dtype=jnp.int32)[None, None, None, :]
    return (starts + slot_ids).astype(jnp.int32)


def setup_inputs(seed: int = 0) -> dict:
    keys = jax.random.split(jax.random.key(seed), 5)
    return {
        "data": draw_data(jax.random.fold_in(keys[4], 71), 0),
        "correlation_index": draw_correlation_index(jax.random.fold_in(keys[4], 71), 0),
        "correlation_count": draw_correlation_count(jax.random.fold_in(keys[4], 71), 0),
        "smoothing": jnp.clip(jnp.exp(jax.random.uniform(keys[3], (3,), jnp.float32, math.log(0.5), math.log(4.0))), 0.5, 4.0),
    }


damping = 0.05
sim_eps = 1e-5


def time_axis(samples):
    return (jnp.arange(samples, dtype=jnp.float32) - (samples - 1) / 2.0) / (samples / 2.0)


def time_slope(trace_rows):
    padded = jnp.pad(trace_rows, [(0, 0)] * (trace_rows.ndim - 1) + [(1, 1)])
    return 0.5 * (padded[..., 2:] - padded[..., :-2])


def corrected(raw_rows, time_shift, log_gain, gain_trend):
    values = raw_rows.astype(jnp.float32)
    time_pos = time_axis(raw_rows.shape[-1])
    amplitude = jnp.exp(log_gain[..., None] + gain_trend[..., None] * time_pos)
    return (amplitude * (values + time_shift[..., None] * time_slope(values))).astype(jnp.bfloat16)


def pair_terms(own_rows, partner_rows, live_mask):
    own_vals = own_rows.astype(jnp.float32)
    partner_vals = partner_rows.astype(jnp.float32)
    time_pos = time_axis(own_vals.shape[-1])
    residual = partner_vals - own_vals
    moved = time_slope(own_vals)
    tilted = time_pos * own_vals
    energy = jnp.mean(own_vals * own_vals, axis=-1)
    cross_term = jnp.mean(own_vals * partner_vals, axis=-1)
    other_energy = jnp.mean(partner_vals * partner_vals, axis=-1)
    weight = live_mask * cross_term * cross_term / ((energy + sim_eps) * (other_energy + sim_eps))
    numerator = jnp.stack([jnp.mean(residual * moved, axis=-1), jnp.mean(residual * own_vals, axis=-1),
                           jnp.mean(residual * tilted, axis=-1)])
    denominator = jnp.stack([jnp.mean(moved * moved, axis=-1), energy, jnp.mean(tilted * tilted, axis=-1)])
    return weight * numerator, weight * denominator


def survey_terms(dest_group, current, correlation_index, correlation_count):
    groups = current.shape[0]
    index_dest = lax.dynamic_index_in_dim(correlation_index, dest_group, axis=2, keepdims=False)
    count_dest = lax.dynamic_index_in_dim(correlation_count, dest_group, axis=2, keepdims=False)
    group_ids = jnp.arange(groups, dtype=jnp.int32)[:, None, None]
    tile_ids = jnp.arange(N_TILE, dtype=jnp.int32)[None, :, None]
    partner_rows = current[group_ids, tile_ids, index_dest]
    own_all = lax.dynamic_index_in_dim(current, dest_group, axis=0, keepdims=False)
    own_rows = own_all[tile_ids, index_dest]
    slot_ids = jnp.arange(CAP, dtype=jnp.int32)
    live_mask = (slot_ids[None, None, :] < count_dest[..., None]).astype(jnp.float32)
    numerator, denominator = pair_terms(own_rows, partner_rows, live_mask)
    empty_sum = jnp.zeros((3, N_TILE, TX * TY), jnp.float32)
    target = empty_sum.at[:, tile_ids, index_dest].add(numerator)
    weights = empty_sum.at[:, tile_ids, index_dest].add(denominator)
    return target.reshape(3, NXTOT, TY), weights.reshape(3, NXTOT, TY)


def smooth_apply(field, weights, smoothing):
    padded = jnp.pad(field, ((0, 0), (0, 0), (1, 1), (1, 1)))
    beside = padded[:, :, 2:, 1:-1] + padded[:, :, :-2, 1:-1] + padded[:, :, 1:-1, 2:] + padded[:, :, 1:-1, :-2]
    strength = smoothing[None, :, None, None]
    return (weights + damping + 4.0 * strength) * field - strength * beside


def conjugate(target, weights, smoothing):
    solution = jnp.zeros_like(target)
    residual = target
    direction = target
    norm_now = jnp.sum(residual * residual, axis=(2, 3))
    for iteration in range(CG_ITERS):
        image = smooth_apply(direction, weights, smoothing)
        alpha = norm_now / jnp.sum(direction * image, axis=(2, 3))
        solution = solution + alpha[:, :, None, None] * direction
        residual = residual - alpha[:, :, None, None] * image
        norm_next = jnp.sum(residual * residual, axis=(2, 3))
        direction = residual + (norm_next / norm_now)[:, :, None, None] * direction
        norm_now = norm_next
    return solution


def reference(data, correlation_index, correlation_count, smoothing):
    groups = data.shape[0]
    stacked = data.reshape(groups, N_TILE, TX * TY, NT)
    fields = jnp.zeros((groups, 3, NXTOT, TY), jnp.float32)
    for outer_round in range(ROUNDS):
        flat_fields = fields.reshape(groups, 3, N_TILE, TX * TY)
        current = corrected(stacked, flat_fields[:, 0], flat_fields[:, 1], flat_fields[:, 2])

        def per_group(dest_group):
            return survey_terms(dest_group, current, correlation_index, correlation_count)

        target, weights = lax.map(per_group, jnp.arange(groups, dtype=jnp.int32))
        fields = fields + conjugate(target, weights, smoothing)
    flat_fields = fields.reshape(groups, 3, N_TILE, TX * TY)
    volume = corrected(stacked, flat_fields[:, 0], flat_fields[:, 1], flat_fields[:, 2])
    return fields, volume.reshape(groups, NXTOT, TY, NT)
```

```python
import functools

import jax
import jax.numpy as jnp
from jax import lax
from jax.experimental import pallas as pl
from jax.experimental.pallas import tpu as pltpu
from jax.sharding import PartitionSpec as P

ROUNDS = 2
CG_ITERS = 3

damping = 0.05
sim_eps = 1e-05

f32 = jnp.float32
VMEM = pl.BlockSpec(memory_space=pltpu.VMEM)
SMEM = pl.BlockSpec(memory_space=pltpu.SMEM)
PARAMS = pltpu.CompilerParams(vmem_limit_bytes=16 * 1024 * 1024)


def partner_of(me, k, n):
    if n & (n - 1) == 0:
        return me ^ k
    return lax.rem(me + k, n)


def sender_to(me, k, n):
    if n & (n - 1) == 0:
        return me ^ k
    return lax.rem(me + n - k, n)


def shift_pairs(k, n):
    if n & (n - 1) == 0:
        return [(i, i ^ k) for i in range(n)]
    return [(i, (i + k) % n) for i in range(n)]


def time_row(samples):
    i = lax.broadcasted_iota(jnp.int32, (1, samples), 1).astype(f32)
    return (i - (samples - 1) / 2.0) / (samples / 2.0)


def slope_matrix(samples):
    row = lax.broadcasted_iota(jnp.int32, (samples, samples), 0)
    col = lax.broadcasted_iota(jnp.int32, (samples, samples), 1)
    up = jnp.where(row == col + 1, 0.5, 0.0)
    down = jnp.where(row == col - 1, 0.5, 0.0)
    return (up - down).astype(jnp.bfloat16)


def eye_mask(rows, lanes):
    row = lax.broadcasted_iota(jnp.int32, (rows, lanes), 0)
    col = lax.broadcasted_iota(jnp.int32, (rows, lanes), 1)
    return row == col


def to_lanes(column, eye):
    return jnp.sum(jnp.where(eye, column, 0.0), axis=0, keepdims=True)


def to_column(row, eye):
    return jnp.sum(jnp.where(eye, row, 0.0), axis=1, keepdims=True)


def window_of(start, total, cap):
    base = jnp.minimum((start // 8) * 8, total - cap - 8)
    return pl.multiple_of(base, 8), start - base


def corrected_rows(raw, shift, gain, trend, slope_mat, time_pos):
    slope = jnp.dot(raw, slope_mat, preferred_element_type=f32)
    amplitude = jnp.exp(gain + trend * time_pos)
    return (amplitude * (raw.astype(f32) + shift * slope)).astype(jnp.bfloat16)


def pack_kernel(n, index_ref, data_ref, *out_refs):
    me = lax.axis_index("survey")
    total, cap = data_ref.shape[0], out_refs[0].shape[0]
    sub = lax.broadcasted_iota(jnp.int32, (8, data_ref.shape[1]), 0)
    for k in range(1, n):
        base, off = window_of(index_ref[me, partner_of(me, k, n)], total, cap)
        out = out_refs[k - 1]
        out[8:, :] = data_ref[pl.ds(base + 8, cap - 8), :]
        first = data_ref[pl.ds(base, 8), :].astype(f32)
        last = data_ref[pl.ds(base + cap, 8), :].astype(f32)
        out[:8, :] = jnp.where(sub >= off, first, last).astype(out.dtype)


def energies(rows, slope_mat, time_pos, eye, scale):
    vals = rows.astype(f32)
    moved = jnp.dot(rows, slope_mat, preferred_element_type=f32)
    tilted = time_pos * vals
    return [
        to_lanes(jnp.sum(part * part, axis=1, keepdims=True) * scale, eye)
        for part in (moved, vals, tilted)
    ]


def own_first_kernel(data_ref, energy_ref):
    rows_x, rows_y = energy_ref.shape[1:]
    samples = data_ref.shape[1]
    slope_mat, time_pos = slope_matrix(samples), time_row(samples)
    eye = eye_mask(rows_y, rows_y)
    for x in range(rows_x):
        rows = data_ref[x * rows_y : (x + 1) * rows_y, :]
        for c, row in enumerate(energies(rows, slope_mat, time_pos, eye, 1.0 / samples)):
            energy_ref[c, x : x + 1, :] = row


def own_next_kernel(data_ref, fields_ref, current_ref, energy_ref):
    rows_x, rows_y = energy_ref.shape[1:]
    samples = data_ref.shape[1]
    slope_mat, time_pos = slope_matrix(samples), time_row(samples)
    eye = eye_mask(rows_y, rows_y)
    for x in range(rows_x):
        block = slice(x * rows_y, (x + 1) * rows_y)
        columns = [to_column(fields_ref[c, x : x + 1, :], eye) for c in range(3)]
        rows = corrected_rows(data_ref[block, :], *columns, slope_mat, time_pos)
        current_ref[block, :] = rows
        for c, row in enumerate(energies(rows, slope_mat, time_pos, eye, 1.0 / samples)):
            energy_ref[c, x : x + 1, :] = row


def pair_kernel(n, second, index_ref, count_ref, own_ref, energy_ref, *refs):
    partner_refs = refs[: n - 1]
    field_refs = refs[n - 1 : 2 * (n - 1)] if second else None
    out_ref = refs[-1]
    me = lax.axis_index("survey")
    total, samples = own_ref.shape
    cap = partner_refs[0].shape[0]
    rows_x, rows_y = energy_ref.shape[1:]
    scale = 1.0 / samples
    slope_mat, time_pos = slope_matrix(samples), time_row(samples)
    eye, eye8 = eye_mask(cap, rows_y), eye_mask(8, rows_y)
    grid_x = lax.broadcasted_iota(jnp.int32, (rows_x, rows_y), 0)
    grid_y = lax.broadcasted_iota(jnp.int32, (rows_x, rows_y), 1)
    position = grid_x * rows_y + grid_y
    energy = energy_ref[1]
    target = [jnp.zeros((rows_x, rows_y), f32) for _ in range(3)]
    similar = jnp.zeros((rows_x, rows_y), f32)
    for k in range(1, n):
        source = sender_to(me, k, n)
        start, count = index_ref[source, me], count_ref[source, me]
        base, off = window_of(start, total, cap)
        first_x = base // rows_y
        first_y = base - first_x * rows_y
        raw = partner_refs[k - 1][...]
        if second:
            lane = lax.broadcasted_iota(jnp.int32, (1, rows_y), 1)
            columns = []
            for c in range(3):
                here = field_refs[k - 1][c, pl.ds(first_x, 1), :]
                after = field_refs[k - 1][c, pl.ds(first_x + 1, 1), :]
                wrapped = jnp.where(lane >= first_y + off, here, after)
                wide = jnp.broadcast_to(wrapped, (8, rows_y))
                wide = pltpu.roll(wide, lax.rem(rows_y - first_y, rows_y), 1)
                columns.append(to_column(wide[:1], eye))
            raw = corrected_rows(raw, *columns, slope_mat, time_pos)
        partner = raw.astype(f32)
        own_rows = own_ref[pl.ds(base, cap + 8), :]
        moved = jnp.dot(own_rows, slope_mat, preferred_element_type=f32)
        own = own_rows.astype(f32)

        def reduced(part_own, part_moved, part_partner, mask):
            residual = part_partner - part_own
            along = residual * part_own
            parts = (
                residual * part_moved,
                along,
                residual * (time_pos * part_own),
                part_own * part_partner,
                part_partner * part_partner,
            )
            return [to_lanes(jnp.sum(q, axis=1, keepdims=True) * scale, mask) for q in parts]

        main = reduced(own[:cap], moved[:cap], partner, eye)
        tail = reduced(own[cap:], moved[cap:], partner[:8], eye8)
        chosen = (grid_x == first_x) | (grid_y < first_y)
        placed = []
        for q in range(5):
            a = pltpu.roll(jnp.broadcast_to(main[q], (rows_x, rows_y)), first_y, 1)
            b = pltpu.roll(jnp.broadcast_to(tail[q], (rows_x, rows_y)), first_y, 1)
            placed.append(jnp.where(chosen, a, b))
        cross_term, other_energy = placed[3], placed[4]
        live = (position >= start) & (position < start + count)
        weight = cross_term * cross_term / ((energy + sim_eps) * (other_energy + sim_eps))
        weight = jnp.where(live, weight, 0.0)
        similar = similar + weight
        for c in range(3):
            target[c] = target[c] + weight * placed[c]
    for c in range(3):
        out_ref[c] = target[c]
        out_ref[3 + c] = similar * energy_ref[c]


def grid_solve(masks, smoothing_ref, piece_refs, grid_ref, tile):
    rows_x = piece_refs[0].shape[1]
    for piece, mask in zip(piece_refs, masks):
        spot = pl.multiple_of((tile ^ mask) * rows_x, rows_x)
        for c in range(6):
            grid_ref[c, pl.ds(spot, rows_x), :] = piece[c]
    size_x, size_y = grid_ref.shape[1:]
    grid_x = lax.broadcasted_iota(jnp.int32, (size_x, size_y), 0)
    grid_y = lax.broadcasted_iota(jnp.int32, (size_x, size_y), 1)

    def total(q):
        return jnp.sum(q, keepdims=True)

    def beside(v):
        return (
            jnp.where(grid_x > 0, pltpu.roll(v, 1, 0), 0.0)
            + jnp.where(grid_x < size_x - 1, pltpu.roll(v, size_x - 1, 0), 0.0)
            + jnp.where(grid_y > 0, pltpu.roll(v, 1, 1), 0.0)
            + jnp.where(grid_y < size_y - 1, pltpu.roll(v, size_y - 1, 1), 0.0)
        )

    updates = []
    for c in range(3):
        strength = smoothing_ref[c]
        diagonal = grid_ref[3 + c] + (damping + 4.0 * strength)
        residual = grid_ref[c]
        direction = residual
        norm_now = total(residual * residual)
        update = None
        for iteration in range(CG_ITERS):
            image = diagonal * direction - strength * beside(direction)
            alpha = norm_now / total(direction * image)
            step = alpha * direction
            update = step if update is None else update + step
            if iteration + 1 < CG_ITERS:
                residual = residual - alpha * image
                norm_next = total(residual * residual)
                direction = residual + (norm_next / norm_now) * direction
                norm_now = norm_next
        updates.append(update)
    return updates


def solve_first_kernel(masks, smoothing_ref, *refs):
    pieces, fields_ref, grid_ref = refs[: len(masks)], refs[-2], refs[-1]
    tile = lax.axis_index("tile")
    updates = grid_solve(masks, smoothing_ref, pieces, grid_ref, tile)
    rows_x = fields_ref.shape[1]
    for c in range(3):
        grid_ref[c] = updates[c]
        fields_ref[c] = grid_ref[c, pl.ds(pl.multiple_of(tile * rows_x, rows_x), rows_x), :]


def solve_last_kernel(masks, smoothing_ref, before_ref, data_ref, *refs):
    pieces, fields_ref, volume_ref, grid_ref = refs[: len(masks)], refs[-3], refs[-2], refs[-1]
    tile = lax.axis_index("tile")
    updates = grid_solve(masks, smoothing_ref, pieces, grid_ref, tile)
    rows_x, rows_y = fields_ref.shape[1:]
    for c in range(3):
        grid_ref[c] = updates[c]
        mine = grid_ref[c, pl.ds(pl.multiple_of(tile * rows_x, rows_x), rows_x), :]
        fields_ref[c] = before_ref[c] + mine
    samples = data_ref.shape[1]
    slope_mat, time_pos = slope_matrix(samples), time_row(samples)
    eye = eye_mask(rows_y, rows_y)
    for x in range(rows_x):
        block = slice(x * rows_y, (x + 1) * rows_y)
        columns = [to_column(fields_ref[c, x : x + 1, :], eye) for c in range(3)]
        volume_ref[block, :] = corrected_rows(data_ref[block, :], *columns, slope_mat, time_pos)


def gather_tiles(piece, n):
    pieces = {0: piece}
    for mask in range(2, n, 2):
        pieces[mask] = lax.ppermute(piece, "tile", [(i, i ^ mask) for i in range(n)])
    if n > 1:
        for mask in list(pieces):
            pieces[mask + 1] = lax.ppermute(pieces[mask], "tile", [(i, i ^ 1) for i in range(n)])
    masks = sorted(pieces)
    return masks, [pieces[m] for m in masks]


def exchange(arrays, n):
    return [lax.ppermute(a, "survey", shift_pairs(k, n)) for k, a in zip(range(1, n), arrays)]


def local(n_survey, n_tile, data, correlation_index, correlation_count, smoothing):
    rows_x, rows_y, samples = data.shape[1:]
    total, cap = rows_x * rows_y, correlation_index.shape[-1]
    raw = data.reshape(total, samples)
    starts = correlation_index[:, 0, :, 0]
    counts = correlation_count[:, 0, :]
    packed = jax.ShapeDtypeStruct((cap, samples), data.dtype)
    field_shape = jax.ShapeDtypeStruct((3, rows_x, rows_y), f32)
    term_shape = jax.ShapeDtypeStruct((6, rows_x, rows_y), f32)
    raw_shape = jax.ShapeDtypeStruct((total, samples), data.dtype)
    grid = pltpu.VMEM((6, rows_x * n_tile, rows_y), f32)

    outgoing = pl.pallas_call(
        functools.partial(pack_kernel, n_survey),
        out_shape=[packed] * (n_survey - 1),
        in_specs=[SMEM, VMEM],
        out_specs=[VMEM] * (n_survey - 1),
        compiler_params=PARAMS,
        name="pack",
    )(starts, raw)
    arrived = exchange(outgoing, n_survey)
    energy = pl.pallas_call(
        own_first_kernel, out_shape=field_shape, in_specs=[VMEM], out_specs=VMEM, compiler_params=PARAMS, name="own_first"
    )(raw)
    terms = pl.pallas_call(
        functools.partial(pair_kernel, n_survey, False),
        out_shape=term_shape,
        in_specs=[SMEM] * 2 + [VMEM] * (n_survey + 1),
        out_specs=VMEM,
        compiler_params=PARAMS,
        name="pair_first",
    )(starts, counts, raw, energy, *arrived)
    masks, pieces = gather_tiles(terms, n_tile)
    fields = pl.pallas_call(
        functools.partial(solve_first_kernel, masks),
        out_shape=field_shape,
        in_specs=[SMEM] + [VMEM] * n_tile,
        out_specs=VMEM,
        scratch_shapes=[grid],
        compiler_params=PARAMS,
        name="solve_first",
    )(smoothing, *pieces)

    partner_fields = exchange([fields] * (n_survey - 1), n_survey)
    current, energy = pl.pallas_call(
        own_next_kernel,
        out_shape=[raw_shape, field_shape],
        in_specs=[VMEM] * 2,
        out_specs=[VMEM] * 2,
        compiler_params=PARAMS,
        name="own_next",
    )(raw, fields)
    terms = pl.pallas_call(
        functools.partial(pair_kernel, n_survey, True),
        out_shape=term_shape,
        in_specs=[SMEM] * 2 + [VMEM] * (2 * n_survey),
        out_specs=VMEM,
        compiler_params=PARAMS,
        name="pair_next",
    )(starts, counts, current, energy, *arrived, *partner_fields)
    masks, pieces = gather_tiles(terms, n_tile)
    fields, volume = pl.pallas_call(
        functools.partial(solve_last_kernel, masks),
        out_shape=[field_shape, raw_shape],
        in_specs=[SMEM] + [VMEM] * (n_tile + 2),
        out_specs=[VMEM] * 2,
        scratch_shapes=[grid],
        compiler_params=PARAMS,
        name="solve_last",
    )(smoothing, fields, raw, *pieces)
    return fields.reshape(1, 3, rows_x, rows_y), volume.reshape(1, rows_x, rows_y, samples)


def solution(mesh):
    placed = (
        P("survey", "tile", None, None),
        P(None, "tile", None, None),
        P(None, "tile", None),
        P(),
    )
    return jax.shard_map(
        functools.partial(local, mesh.shape["survey"], mesh.shape["tile"]),
        mesh=mesh,
        in_specs=placed,
        out_specs=(P("survey", None, "tile", None), P("survey", "tile", None, None)),
        check_vma=False,
    )
```

```python
import functools

import jax
import jax.numpy as jnp
from jax import lax
from jax.experimental import pallas as pl
from jax.experimental.pallas import tpu as pltpu
from jax.sharding import PartitionSpec as P

ROUNDS = 2
CG_ITERS = 3

damping = 0.05
sim_eps = 1e-05

f32 = jnp.float32
bf16 = jnp.bfloat16
VMEM = pl.BlockSpec(memory_space=pltpu.VMEM)
ANY = pl.BlockSpec(memory_space=pl.ANY)
PARAMS = pltpu.CompilerParams(vmem_limit_bytes=16 * 1024 * 1024)
NT = (((1,), (1,)), ((), ()))


def is_power(n):
    return n & (n - 1) == 0


def receiver(me, k, n):
    return me ^ k if is_power(n) else lax.rem(me + k, n)


def sender(me, k, n):
    return me ^ k if is_power(n) else lax.rem(me + n - k, n)


def survey_pairs(k, n):
    return [(i, i ^ k if is_power(n) else (i + k) % n) for i in range(n)]


def iota(shape, dim):
    return lax.broadcasted_iota(jnp.int32, shape, dim)


def time_of(sample, samples):
    return (sample.astype(f32) - (samples - 1) / 2.0) / (samples / 2.0)


def time_column(samples, lanes):
    return time_of(iota((samples, lanes), 0), samples)


def joined_blocks(data_ref, start, rows_x, rows_y):
    block = start // rows_y
    split = start - block * rows_y
    after = jnp.minimum(block + 1, rows_x - 1)
    here = data_ref[pl.ds(pl.multiple_of(block * rows_y, rows_y), rows_y), :].astype(f32)
    there = data_ref[pl.ds(pl.multiple_of(after * rows_y, rows_y), rows_y), :].astype(f32)
    return jnp.where(iota(here.shape, 0) >= split, here, there).astype(data_ref.dtype)


def pack_kernel(n, rows_x, index_ref, data_ref, *out_refs):
    me = lax.axis_index("survey")
    rows_y = data_ref.shape[0] // rows_x
    for k in range(1, n):
        start = jnp.min(index_ref[me, pl.ds(receiver(me, k, n), 1), :])
        out_refs[k - 1][...] = joined_blocks(data_ref, start, rows_x, rows_y)


def put_rows(ref, k, rows):
    for i, row in enumerate(rows):
        ref[k, i : i + 1, :] = row


def mean_over(values):
    return jnp.sum(values, axis=0, keepdims=True) * (1.0 / values.shape[0])


def energy_rows(vals, moved, time_pos):
    tilted = time_pos * vals
    return [mean_over(moved * moved), mean_over(vals * vals), mean_over(tilted * tilted)]


def prepare_kernel(n, index_ref, count_ref, data_ref, basis_ref, own_ref, moved_ref, mask_ref, energy_ref):
    me = lax.axis_index("survey")
    samples, rows_y = own_ref.shape[1:]
    rows_x = data_ref.shape[0] // rows_y
    row, col = iota((samples, samples), 0), iota((samples, samples), 1)
    basis_ref[:samples, :] = jnp.where(row == col, 1.0, 0.0).astype(bf16)
    basis_ref[samples:, :] = (jnp.where(col == row + 1, 0.5, 0.0) - jnp.where(col == row - 1, 0.5, 0.0)).astype(bf16)
    time_pos = time_column(samples, rows_y)
    position = iota((rows_x, rows_y), 0) * rows_y + iota((rows_x, rows_y), 1)
    for k in range(1, n):
        source = sender(me, k, n)
        start = jnp.min(index_ref[source, pl.ds(me, 1), :])
        counts = count_ref[source]
        count = jnp.sum(jnp.where(iota(counts.shape, 1) == me, counts, 0))
        mask_ref[k - 1] = jnp.where((position >= start) & (position < start + count), 1.0, 0.0)
        rows = joined_blocks(data_ref, start, rows_x, rows_y)
        both = lax.dot_general(basis_ref[...], rows, NT, preferred_element_type=f32)
        own_ref[k - 1] = both[:samples]
        moved_ref[k - 1] = both[samples:]
        put_rows(energy_ref, k - 1, energy_rows(both[:samples], both[samples:], time_pos))


def corrected_lanes(values, moved, fields_ref, mask, time_pos):
    shift, gain, trend = [jnp.sum(fields_ref[c] * mask, axis=0, keepdims=True) for c in range(3)]
    amplitude = jnp.exp(gain + trend * time_pos)
    return (amplitude * (values + shift * moved)).astype(bf16)


def refresh_kernel(n, fields_ref, basis_ref, own_ref, moved_ref, mask_ref, *refs):
    arrived = refs[: n - 1]
    new_own_ref, new_moved_ref, energy_ref, partner_ref, partner_moved_ref = refs[n - 1 :]
    samples, rows_y = own_ref.shape[1:]
    time_pos = time_column(samples, rows_y)
    for k in range(n - 1):
        rounded = corrected_lanes(own_ref[k], moved_ref[k], fields_ref, mask_ref[k], time_pos)
        vals = rounded.astype(f32)
        moved = jnp.dot(basis_ref[samples:, :], rounded, preferred_element_type=f32)
        new_own_ref[k] = vals
        new_moved_ref[k] = moved
        put_rows(energy_ref, k, energy_rows(vals, moved, time_pos))
        both = lax.dot_general(basis_ref[...], arrived[k][...], NT, preferred_element_type=f32)
        partner_ref[k] = both[:samples]
        partner_moved_ref[k] = both[samples:]


def add_pair(sums, own, moved, partner, mask, energy_ref, k, time_pos):
    residual = partner - own
    along = residual * own
    slope_sum = mean_over(residual * moved)
    gain_sum = mean_over(along)
    trend_sum = mean_over(time_pos * along)
    cross_term = mean_over(own * partner)
    other_energy = mean_over(partner * partner)
    energy = [energy_ref[k, i : i + 1, :] for i in range(3)]
    weight = cross_term * cross_term / ((energy[1] + sim_eps) * (other_energy + sim_eps))
    for c, row in enumerate([slope_sum, gain_sum, trend_sum] + energy):
        term = mask * (weight * row)
        sums[c] = term if sums[c] is None else sums[c] + term


def pair_first_kernel(n, basis_ref, own_ref, moved_ref, mask_ref, energy_ref, *refs):
    arrived, out_ref = refs[: n - 1], refs[-1]
    samples, rows_y = own_ref.shape[1:]
    time_pos = time_column(samples, rows_y)
    sums = [None] * 6
    for k in range(n - 1):
        partner = lax.dot_general(basis_ref[:samples, :], arrived[k][...], NT, preferred_element_type=f32)
        add_pair(sums, own_ref[k], moved_ref[k], partner, mask_ref[k], energy_ref, k, time_pos)
    for c in range(6):
        out_ref[c] = sums[c]


def pair_next_kernel(n, own_ref, moved_ref, mask_ref, energy_ref, partner_ref, partner_moved_ref, *refs):
    field_refs, out_ref = refs[: n - 1], refs[-1]
    samples, rows_y = own_ref.shape[1:]
    time_pos = time_column(samples, rows_y)
    sums = [None] * 6
    for k in range(n - 1):
        partner = corrected_lanes(partner_ref[k], partner_moved_ref[k], field_refs[k], mask_ref[k], time_pos)
        add_pair(sums, own_ref[k], moved_ref[k], partner.astype(f32), mask_ref[k], energy_ref, k, time_pos)
    for c in range(6):
        out_ref[c] = sums[c]


def grid_solve(masks, smoothing_ref, piece_refs, grid_ref, tile):
    rows_x = piece_refs[0].shape[1]
    for piece, mask in zip(piece_refs, masks):
        spot = pl.multiple_of((tile ^ mask) * rows_x, rows_x)
        for c in range(6):
            grid_ref[c, pl.ds(spot, rows_x), :] = piece[c]
    size_x, size_y = grid_ref.shape[1:]
    grid_x = iota((size_x, size_y), 0)
    grid_y = iota((size_x, size_y), 1)
    each = range(3)

    def total(q):
        return jnp.sum(jnp.sum(q, axis=0, keepdims=True), axis=1, keepdims=True)

    def beside(v):
        return (
            jnp.where(grid_x > 0, pltpu.roll(v, 1, 0), 0.0)
            + jnp.where(grid_x < size_x - 1, pltpu.roll(v, size_x - 1, 0), 0.0)
            + jnp.where(grid_y > 0, pltpu.roll(v, 1, 1), 0.0)
            + jnp.where(grid_y < size_y - 1, pltpu.roll(v, size_y - 1, 1), 0.0)
        )

    strength = [smoothing_ref[0:1, c : c + 1] for c in each]
    diagonal = [grid_ref[3 + c] + (damping + 4.0 * strength[c]) for c in each]

    def apply(v):
        near = [beside(v[c]) for c in each]
        return [diagonal[c] * v[c] - strength[c] * near[c] for c in each]

    residual = [grid_ref[c] for c in each]
    image = apply(residual)
    norm_now = [total(residual[c] * residual[c]) for c in each]
    product = [total(residual[c] * image[c]) for c in each]
    alpha = [norm_now[c] / product[c] for c in each]
    direction, along = residual, image
    update = [alpha[c] * direction[c] for c in each]
    for iteration in range(1, CG_ITERS):
        residual = [residual[c] - alpha[c] * along[c] for c in each]
        image = apply(residual)
        norm_next = [total(residual[c] * residual[c]) for c in each]
        product = [total(residual[c] * image[c]) for c in each]
        ratio = [norm_next[c] / norm_now[c] for c in each]
        alpha = [norm_next[c] / (product[c] - ratio[c] * norm_next[c] / alpha[c]) for c in each]
        direction = [residual[c] + ratio[c] * direction[c] for c in each]
        if iteration + 1 < CG_ITERS:
            along = [image[c] + ratio[c] * along[c] for c in each]
        update = [update[c] + alpha[c] * direction[c] for c in each]
        norm_now = norm_next
    return update


def own_part(updates, grid_ref, tile, rows_x):
    for c in range(3):
        grid_ref[c] = updates[c]
    spot = pl.ds(pl.multiple_of(tile * rows_x, rows_x), rows_x)
    return [grid_ref[c, spot, :] for c in range(3)]


def solve_first_kernel(masks, smoothing_ref, *refs):
    pieces, fields_ref, grid_ref = refs[: len(masks)], refs[-2], refs[-1]
    tile = lax.axis_index("tile")
    updates = grid_solve(masks, smoothing_ref, pieces, grid_ref, tile)
    for c, mine in enumerate(own_part(updates, grid_ref, tile, fields_ref.shape[1])):
        fields_ref[c] = mine


def three_parts(values):
    parts = []
    for _ in range(3):
        part = values.astype(bf16).astype(f32)
        parts.append(part)
        values = values - part
    return parts


def solve_last_kernel(masks, smoothing_ref, before_ref, data_ref, basis_ref, *refs):
    pieces = refs[: len(masks)]
    fields_ref, volume_ref, grid_ref, block_ref, sems = refs[len(masks) :]
    tile = lax.axis_index("tile")
    updates = grid_solve(masks, smoothing_ref, pieces, grid_ref, tile)
    rows_x, rows_y = fields_ref.shape[1:]
    samples = data_ref.shape[1]
    parts = []
    for c, mine in enumerate(own_part(updates, grid_ref, tile, rows_x)):
        mine = before_ref[c] + mine
        fields_ref[c] = mine
        parts += three_parts(mine)
    lanes = 16 * rows_x
    parts.append(jnp.zeros((lanes - 9 * rows_x, rows_y), f32))
    columns = jnp.transpose(jnp.concatenate(parts, axis=0))
    kind = iota((lanes, samples), 0) // rows_x
    spread_shift = jnp.where(kind < 3, 1.0, 0.0).astype(bf16)
    time_pos = time_of(iota((lanes, samples), 1), samples)
    spread_power = jnp.where((kind >= 3) & (kind < 6), 1.0, jnp.where((kind >= 6) & (kind < 9), time_pos, 0.0)).astype(bf16)
    which = lax.rem(iota((rows_y, lanes), 1), rows_x)
    copies = []
    for x in range(rows_x):
        rows = slice(x * rows_y, (x + 1) * rows_y)
        mine = jnp.where(which == x, columns, 0.0).astype(bf16)
        shift = jnp.dot(mine, spread_shift, preferred_element_type=f32)
        power = jnp.dot(mine, spread_power, preferred_element_type=f32)
        raw = data_ref[rows, :]
        slope = lax.dot_general(raw, basis_ref[samples:, :], NT, preferred_element_type=f32)
        block_ref[rows, :] = (jnp.exp(power) * (raw.astype(f32) + shift * slope)).astype(volume_ref.dtype)
        copy = pltpu.make_async_copy(block_ref.at[rows, :], volume_ref.at[rows, :], sems.at[x])
        copy.start()
        copies.append(copy)
    for copy in copies:
        copy.wait()


def gather_tiles(piece, n):
    if not is_power(n):
        every = lax.all_gather(piece, "tile")
        me = lax.axis_index("tile")
        return list(range(n)), [lax.dynamic_index_in_dim(every, me ^ m, keepdims=False) for m in range(n)]
    pieces = {0: piece}
    for mask in range(2, n, 2):
        pieces[mask] = lax.ppermute(piece, "tile", [(i, i ^ mask) for i in range(n)])
    if n > 1:
        for mask in list(pieces):
            pieces[mask + 1] = lax.ppermute(pieces[mask], "tile", [(i, i ^ 1) for i in range(n)])
    masks = sorted(pieces)
    return masks, [pieces[m] for m in masks]


def exchange(arrays, n):
    return [lax.ppermute(a, "survey", survey_pairs(k, n)) for k, a in zip(range(1, n), arrays)]


def call(kernel, name, out_shape, n_in, **options):
    single = not isinstance(out_shape, list)
    options = {"out_specs": VMEM if single else [VMEM] * len(out_shape), **options}
    return pl.pallas_call(
        kernel,
        out_shape=out_shape,
        in_specs=[VMEM] * n_in,
        compiler_params=PARAMS,
        name=name,
        **options,
    )


def local(n_survey, n_tile, data, correlation_index, correlation_count, smoothing):
    rows_x, rows_y, samples = data.shape[1:]
    total, cap = rows_x * rows_y, correlation_index.shape[-1]
    assert cap <= rows_y and is_power(n_tile)
    others = n_survey - 1
    raw = data.reshape(total, samples)
    index = correlation_index[:, 0]
    smoothing = smoothing.reshape(1, 3)
    packed = jax.ShapeDtypeStruct((rows_y, samples), data.dtype)
    field_shape = jax.ShapeDtypeStruct((3, rows_x, rows_y), f32)
    term_shape = jax.ShapeDtypeStruct((6, rows_x, rows_y), f32)
    lane_shape = jax.ShapeDtypeStruct((others, samples, rows_y), f32)
    mask_shape = jax.ShapeDtypeStruct((others, rows_x, rows_y), f32)
    energy_shape = jax.ShapeDtypeStruct((others, 8, rows_y), f32)
    basis_shape = jax.ShapeDtypeStruct((2 * samples, samples), bf16)
    volume_shape = jax.ShapeDtypeStruct((total, samples), data.dtype)
    grid = pltpu.VMEM((6, rows_x * n_tile, rows_y), f32)

    outgoing = call(functools.partial(pack_kernel, n_survey, rows_x), "pack", [packed] * others, 2)(index, raw)
    arrived = exchange(outgoing, n_survey)
    basis, own, moved, mask, energy = call(
        functools.partial(prepare_kernel, n_survey),
        "prepare",
        [basis_shape, lane_shape, lane_shape, mask_shape, energy_shape],
        3,
    )(index, correlation_count, raw)
    terms = call(functools.partial(pair_first_kernel, n_survey), "pair_first", term_shape, 5 + others)(
        basis, own, moved, mask, energy, *arrived
    )
    masks, pieces = gather_tiles(terms, n_tile)
    fields = call(
        functools.partial(solve_first_kernel, masks), "solve_first", field_shape, 1 + n_tile, scratch_shapes=[grid]
    )(smoothing, *pieces)

    partner_fields = exchange([fields] * others, n_survey)
    own, moved, energy, partner, partner_moved = call(
        functools.partial(refresh_kernel, n_survey),
        "refresh",
        [lane_shape, lane_shape, energy_shape, lane_shape, lane_shape],
        5 + others,
    )(fields, basis, own, moved, mask, *arrived)
    terms = call(functools.partial(pair_next_kernel, n_survey), "pair_next", term_shape, 6 + others)(
        own, moved, mask, energy, partner, partner_moved, *partner_fields
    )
    masks, pieces = gather_tiles(terms, n_tile)
    fields, volume = call(
        functools.partial(solve_last_kernel, masks),
        "solve_last",
        [field_shape, volume_shape],
        4 + n_tile,
        out_specs=[VMEM, ANY],
        scratch_shapes=[grid, pltpu.VMEM((total, samples), data.dtype), pltpu.SemaphoreType.DMA((rows_x,))],
    )(smoothing, fields, raw, basis, *pieces)
    return fields.reshape(1, 3, rows_x, rows_y), volume.reshape(1, rows_x, rows_y, samples)


def solution(mesh):
    placed = (
        P("survey", "tile", None, None),
        P(None, "tile", None, None),
        P(None, "tile", None),
        P(),
    )
    return jax.shard_map(
        functools.partial(local, mesh.shape["survey"], mesh.shape["tile"]),
        mesh=mesh,
        in_specs=placed,
        out_specs=(P("survey", None, "tile", None), P("survey", "tile", None, None)),
        check_vma=False,
    )
```

```python
import functools

import jax
import jax.numpy as jnp
from jax import lax
from jax.experimental import pallas as pl
from jax.experimental.pallas import tpu as pltpu
from jax.sharding import PartitionSpec as P


CG_ITERS = 3

damping = 0.05
sim_eps = 1e-05

f32 = jnp.float32
bf16 = jnp.bfloat16
VMEM = pl.BlockSpec(memory_space=pltpu.VMEM)
ANY = pl.BlockSpec(memory_space=pl.ANY)
PARAMS = pltpu.CompilerParams(vmem_limit_bytes=16 * 1024 * 1024)
NT = (((1,), (1,)), ((), ()))


def is_power(n):
    return n & (n - 1) == 0


def receiver(me, k, n):
    return me ^ k if is_power(n) else lax.rem(me + k, n)


def sender(me, k, n):
    return me ^ k if is_power(n) else lax.rem(me + n - k, n)


def survey_pairs(k, n):
    return [(i, i ^ k if is_power(n) else (i + k) % n) for i in range(n)]


def iota(shape, dim):
    return lax.broadcasted_iota(jnp.int32, shape, dim)


def time_of(sample, samples):
    return (sample.astype(f32) - (samples - 1) / 2.0) / (samples / 2.0)


def time_column(samples, lanes):
    return time_of(iota((samples, lanes), 0), samples)


def joined_blocks(data_ref, start, rows_x, rows_y):
    block = start // rows_y
    split = start - block * rows_y
    after = jnp.minimum(block + 1, rows_x - 1)
    here = data_ref[pl.ds(pl.multiple_of(block * rows_y, rows_y), rows_y), :].astype(f32)
    there = data_ref[pl.ds(pl.multiple_of(after * rows_y, rows_y), rows_y), :].astype(f32)
    return jnp.where(iota(here.shape, 0) >= split, here, there).astype(data_ref.dtype)


def pack_kernel(n, rows_x, index_ref, data_ref, *out_refs):
    me = lax.axis_index("survey")
    rows_y = data_ref.shape[0] // rows_x
    for k in range(1, n):
        start = jnp.min(index_ref[me, pl.ds(receiver(me, k, n), 1), :])
        out_refs[k - 1][...] = joined_blocks(data_ref, start, rows_x, rows_y)


def put_rows(ref, k, rows):
    for i, row in enumerate(rows):
        ref[k, i : i + 1, :] = row


def mean_over(values):
    return jnp.sum(values, axis=0, keepdims=True) * (1.0 / values.shape[0])


def energy_rows(vals, moved, time_pos):
    tilted = time_pos * vals
    return [mean_over(moved * moved), mean_over(vals * vals), mean_over(tilted * tilted)]


def prepare_kernel(n, index_ref, count_ref, data_ref, basis_ref, own_ref, moved_ref, mask_ref, energy_ref, slope_ref):
    me = lax.axis_index("survey")
    samples, rows_y = own_ref.shape[1:]
    rows_x = data_ref.shape[0] // rows_y
    row, col = iota((samples, samples), 0), iota((samples, samples), 1)
    basis_ref[:samples, :] = jnp.where(row == col, 1.0, 0.0).astype(bf16)
    basis_ref[samples:, :] = (jnp.where(col == row + 1, 0.5, 0.0) - jnp.where(col == row - 1, 0.5, 0.0)).astype(bf16)
    time_pos = time_column(samples, rows_y)
    position = iota((rows_x, rows_y), 0) * rows_y + iota((rows_x, rows_y), 1)
    for k in range(1, n):
        source = sender(me, k, n)
        start = jnp.min(index_ref[source, pl.ds(me, 1), :])
        counts = count_ref[source]
        count = jnp.sum(jnp.where(iota(counts.shape, 1) == me, counts, 0))
        mask_ref[k - 1] = jnp.where((position >= start) & (position < start + count), 1.0, 0.0)
        rows = joined_blocks(data_ref, start, rows_x, rows_y)
        both = lax.dot_general(basis_ref[...], rows, NT, preferred_element_type=f32)
        own_ref[k - 1] = both[:samples]
        moved_ref[k - 1] = both[samples:]
        put_rows(energy_ref, k - 1, energy_rows(both[:samples], both[samples:], time_pos))
    for x in range(rows_x):
        block = slice(x * rows_y, (x + 1) * rows_y)
        slope_ref[block, :] = lax.dot_general(data_ref[block, :], basis_ref[samples:, :], NT, preferred_element_type=f32)


def corrected_lanes(values, moved, fields_ref, mask, time_pos):
    shift, gain, trend = [jnp.sum(fields_ref[c] * mask, axis=0, keepdims=True) for c in range(3)]
    amplitude = jnp.exp(gain + trend * time_pos)
    return (amplitude * (values + shift * moved)).astype(bf16)


def refresh_kernel(n, fields_ref, basis_ref, own_ref, moved_ref, mask_ref, *refs):
    arrived = refs[: n - 1]
    new_own_ref, new_moved_ref, energy_ref, partner_ref, partner_moved_ref = refs[n - 1 :]
    samples, rows_y = own_ref.shape[1:]
    time_pos = time_column(samples, rows_y)
    for k in range(n - 1):
        rounded = corrected_lanes(own_ref[k], moved_ref[k], fields_ref, mask_ref[k], time_pos)
        vals = rounded.astype(f32)
        moved = jnp.dot(basis_ref[samples:, :], rounded, preferred_element_type=f32)
        new_own_ref[k] = vals
        new_moved_ref[k] = moved
        put_rows(energy_ref, k, energy_rows(vals, moved, time_pos))
        both = lax.dot_general(basis_ref[...], arrived[k][...], NT, preferred_element_type=f32)
        partner_ref[k] = both[:samples]
        partner_moved_ref[k] = both[samples:]


def add_pair(sums, own, moved, partner, mask, energy_ref, k, time_pos):
    residual = partner - own
    along = residual * own
    slope_sum = mean_over(residual * moved)
    gain_sum = mean_over(along)
    trend_sum = mean_over(time_pos * along)
    cross_term = mean_over(own * partner)
    other_energy = mean_over(partner * partner)
    energy = [energy_ref[k, i : i + 1, :] for i in range(3)]
    weight = cross_term * cross_term / ((energy[1] + sim_eps) * (other_energy + sim_eps))
    for c, row in enumerate([slope_sum, gain_sum, trend_sum] + energy):
        term = mask * (weight * row)
        sums[c] = term if sums[c] is None else sums[c] + term


def pair_first_kernel(n, basis_ref, own_ref, moved_ref, mask_ref, energy_ref, *refs):
    arrived, out_ref = refs[: n - 1], refs[-1]
    samples, rows_y = own_ref.shape[1:]
    time_pos = time_column(samples, rows_y)
    sums = [None] * 6
    for k in range(n - 1):
        partner = lax.dot_general(basis_ref[:samples, :], arrived[k][...], NT, preferred_element_type=f32)
        add_pair(sums, own_ref[k], moved_ref[k], partner, mask_ref[k], energy_ref, k, time_pos)
    for c in range(6):
        out_ref[c] = sums[c]


def pair_next_kernel(n, own_ref, moved_ref, mask_ref, energy_ref, partner_ref, partner_moved_ref, *refs):
    field_refs, out_ref = refs[: n - 1], refs[-1]
    samples, rows_y = own_ref.shape[1:]
    time_pos = time_column(samples, rows_y)
    sums = [None] * 6
    for k in range(n - 1):
        partner = corrected_lanes(partner_ref[k], partner_moved_ref[k], field_refs[k], mask_ref[k], time_pos)
        add_pair(sums, own_ref[k], moved_ref[k], partner.astype(f32), mask_ref[k], energy_ref, k, time_pos)
    for c in range(6):
        out_ref[c] = sums[c]


def grid_solve(masks, smoothing_ref, piece_refs, grid_ref, tile):
    rows_x = piece_refs[0].shape[1]
    for piece, mask in zip(piece_refs, masks):
        spot = pl.multiple_of((tile ^ mask) * rows_x, rows_x)
        for c in range(6):
            grid_ref[c, pl.ds(spot, rows_x), :] = piece[c]
    size_x, size_y = grid_ref.shape[1:]
    grid_x = iota((size_x, size_y), 0)
    grid_y = iota((size_x, size_y), 1)
    each = range(3)

    def total(q):
        return jnp.sum(jnp.sum(q, axis=0, keepdims=True), axis=1, keepdims=True)

    def beside(v):
        return (
            jnp.where(grid_x > 0, pltpu.roll(v, 1, 0), 0.0)
            + jnp.where(grid_x < size_x - 1, pltpu.roll(v, size_x - 1, 0), 0.0)
            + jnp.where(grid_y > 0, pltpu.roll(v, 1, 1), 0.0)
            + jnp.where(grid_y < size_y - 1, pltpu.roll(v, size_y - 1, 1), 0.0)
        )

    strength = [smoothing_ref[0:1, c : c + 1] for c in each]
    diagonal = [grid_ref[3 + c] + (damping + 4.0 * strength[c]) for c in each]

    def apply(v):
        near = [beside(v[c]) for c in each]
        return [diagonal[c] * v[c] - strength[c] * near[c] for c in each]

    residual = [grid_ref[c] for c in each]
    image = apply(residual)
    norm_now = [total(residual[c] * residual[c]) for c in each]
    product = [total(residual[c] * image[c]) for c in each]
    alpha = [norm_now[c] / product[c] for c in each]
    direction, along = residual, image
    update = [alpha[c] * direction[c] for c in each]
    for iteration in range(1, CG_ITERS):
        residual = [residual[c] - alpha[c] * along[c] for c in each]
        image = apply(residual)
        norm_next = [total(residual[c] * residual[c]) for c in each]
        product = [total(residual[c] * image[c]) for c in each]
        ratio = [norm_next[c] / norm_now[c] for c in each]
        alpha = [norm_next[c] / (product[c] - ratio[c] * norm_next[c] / alpha[c]) for c in each]
        direction = [residual[c] + ratio[c] * direction[c] for c in each]
        if iteration + 1 < CG_ITERS:
            along = [image[c] + ratio[c] * along[c] for c in each]
        update = [update[c] + alpha[c] * direction[c] for c in each]
        norm_now = norm_next
    return update


def tile_part(grid_ref, c, tile, rows_x):
    return grid_ref[c, pl.ds(pl.multiple_of(tile * rows_x, rows_x), rows_x), :]


def solve_first_kernel(masks, smoothing_ref, *refs):
    pieces = refs[: len(masks)]
    fields_ref, beside_ref, grid_ref = refs[len(masks) :]
    tile = lax.axis_index("tile")
    updates = grid_solve(masks, smoothing_ref, pieces, grid_ref, tile)
    for c in range(3):
        grid_ref[c] = updates[c]
        fields_ref[c] = tile_part(grid_ref, c, tile, fields_ref.shape[1])
        beside_ref[c] = tile_part(grid_ref, c, tile ^ 1, fields_ref.shape[1])


def three_parts(values):
    parts = []
    for _ in range(3):
        part = values.astype(bf16).astype(f32)
        parts.append(part)
        values = values - part
    return parts


def solve_last_kernel(masks, smoothing_ref, before_ref, data_ref, slope_ref, *refs):
    pieces = refs[: len(masks)]
    fields_ref, volume_ref, grid_ref, block_ref, sems = refs[len(masks) :]
    tile = lax.axis_index("tile")
    rows_x, rows_y = fields_ref.shape[1:]
    samples = data_ref.shape[1]
    lanes = 16 * rows_x
    kind = iota((lanes, samples), 0) // rows_x
    time_pos = time_of(iota((lanes, samples), 1), samples)
    spread_power = jnp.where((kind >= 3) & (kind < 6), 1.0, jnp.where((kind >= 6) & (kind < 9), time_pos, 0.0))
    spread_shift = jnp.where(kind < 3, 1.0, 0.0)
    spread = jnp.concatenate([spread_shift, spread_power], axis=1).astype(bf16)
    which = lax.rem(iota((rows_y, lanes), 1), rows_x)
    updates = grid_solve(masks, smoothing_ref, pieces, grid_ref, tile)
    parts = []
    for c in range(3):
        grid_ref[c] = updates[c]
        mine = before_ref[c] + tile_part(grid_ref, c, tile, rows_x)
        fields_ref[c] = mine
        parts += three_parts(mine)
    parts.append(jnp.zeros((lanes - 9 * rows_x, rows_y), f32))
    columns = jnp.transpose(jnp.concatenate(parts, axis=0))
    copies = []
    for x in range(rows_x):
        rows = slice(x * rows_y, (x + 1) * rows_y)
        mine = jnp.where(which == x, columns, 0.0).astype(bf16)
        both = jnp.dot(mine, spread, preferred_element_type=f32)
        shift, power = both[:, :samples], both[:, samples:]
        moved = data_ref[rows, :].astype(f32) + shift * slope_ref[rows, :]
        block_ref[rows, :] = (jnp.exp(power) * moved).astype(volume_ref.dtype)
        copy = pltpu.make_async_copy(block_ref.at[rows, :], volume_ref.at[rows, :], sems.at[x])
        copy.start()
        copies.append(copy)
    for copy in copies:
        copy.wait()


def gather_tiles(piece, n):
    pieces = {0: piece}
    for mask in range(3, n, 2):
        pieces[mask] = lax.ppermute(piece, "tile", [(i, i ^ mask) for i in range(n)])
    if n > 1:
        for mask in list(pieces):
            pieces[mask ^ 1] = lax.ppermute(pieces[mask], "tile", [(i, i ^ 1) for i in range(n)])
    masks = sorted(pieces)
    return masks, [pieces[m] for m in masks]


def exchange(arrays, n):
    got = []
    for k in range(1, n):
        got.append(lax.ppermute(arrays[k - 1], "survey", survey_pairs(k, n)))
    return got


def exchange_across(array, n, n_tile):
    got = []
    for k in range(1, n):
        pairs = [(s * n_tile + t, d * n_tile + (t ^ 1)) for s, d in survey_pairs(k, n) for t in range(n_tile)]
        got.append(lax.ppermute(array, ("survey", "tile"), pairs))
    return got


def call(kernel, out_shape, n_in, **options):
    single = not isinstance(out_shape, list)
    options = {"out_specs": VMEM if single else [VMEM] * len(out_shape), **options}
    return pl.pallas_call(kernel, out_shape=out_shape, in_specs=[VMEM] * n_in, compiler_params=PARAMS, **options)


def local(n_survey, n_tile, data, correlation_index, correlation_count, smoothing):
    rows_x, rows_y, samples = data.shape[1:]
    total, cap = rows_x * rows_y, correlation_index.shape[-1]
    assert cap <= rows_y and samples <= 256 and is_power(samples) and is_power(n_tile) and n_tile > 1
    others = n_survey - 1
    raw = data.reshape(total, samples)
    index = correlation_index[:, 0]
    smoothing = smoothing.reshape(1, 3)
    packed = jax.ShapeDtypeStruct((rows_y, samples), data.dtype)
    field_shape = jax.ShapeDtypeStruct((3, rows_x, rows_y), f32)
    term_shape = jax.ShapeDtypeStruct((6, rows_x, rows_y), f32)
    lane_shape = jax.ShapeDtypeStruct((others, samples, rows_y), f32)
    mask_shape = jax.ShapeDtypeStruct((others, rows_x, rows_y), f32)
    energy_shape = jax.ShapeDtypeStruct((others, 8, rows_y), f32)
    basis_shape = jax.ShapeDtypeStruct((2 * samples, samples), bf16)
    slope_shape = jax.ShapeDtypeStruct((total, samples), f32)
    volume_shape = jax.ShapeDtypeStruct((total, samples), data.dtype)
    grid = pltpu.VMEM((6, rows_x * n_tile, rows_y), f32)

    outgoing = call(functools.partial(pack_kernel, n_survey, rows_x), [packed] * others, 2)(index, raw)
    arrived = exchange(outgoing, n_survey)
    basis, own, moved, mask, energy, slope = call(
        functools.partial(prepare_kernel, n_survey),
        [basis_shape, lane_shape, lane_shape, mask_shape, energy_shape, slope_shape],
        3,
    )(index, correlation_count, raw)
    terms = call(functools.partial(pair_first_kernel, n_survey), term_shape, 5 + others)(
        basis, own, moved, mask, energy, *arrived
    )
    masks, pieces = gather_tiles(terms, n_tile)
    fields, beside = call(
        functools.partial(solve_first_kernel, masks), [field_shape] * 2, 1 + n_tile, scratch_shapes=[grid]
    )(smoothing, *pieces)

    partner_fields = exchange_across(beside, n_survey, n_tile)
    own, moved, energy, partner, partner_moved = call(
        functools.partial(refresh_kernel, n_survey),
        [lane_shape, lane_shape, energy_shape, lane_shape, lane_shape],
        5 + others,
    )(fields, basis, own, moved, mask, *arrived)
    terms = call(functools.partial(pair_next_kernel, n_survey), term_shape, 6 + others)(
        own, moved, mask, energy, partner, partner_moved, *partner_fields
    )
    masks, pieces = gather_tiles(terms, n_tile)
    fields, volume = call(
        functools.partial(solve_last_kernel, masks),
        [field_shape, volume_shape],
        4 + n_tile,
        out_specs=[VMEM, ANY],
        scratch_shapes=[grid, pltpu.VMEM((total, samples), data.dtype), pltpu.SemaphoreType.DMA((rows_x,))],
    )(smoothing, fields, raw, slope, *pieces)
    return fields.reshape(1, 3, rows_x, rows_y), volume.reshape(1, rows_x, rows_y, samples)


def solution(mesh):
    placed = (
        P("survey", "tile", None, None),
        P(None, "tile", None, None),
        P(None, "tile", None),
        P(),
    )
    return jax.shard_map(
        functools.partial(local, mesh.shape["survey"], mesh.shape["tile"]),
        mesh=mesh,
        in_specs=placed,
        out_specs=(P("survey", None, "tile", None), P("survey", "tile", None, None)),
        check_vma=False,
    )
```

```python
import functools

import jax
import jax.numpy as jnp
from jax import lax
from jax.experimental import pallas as pl
from jax.experimental.pallas import tpu as pltpu
from jax.sharding import PartitionSpec as P


CG_ITERS = 3

damping = 0.05
sim_eps = 1e-05

f32 = jnp.float32
bf16 = jnp.bfloat16
VMEM = pl.BlockSpec(memory_space=pltpu.VMEM)
ANY = pl.BlockSpec(memory_space=pl.ANY)
HBM = pl.BlockSpec(memory_space=pltpu.HBM)
PARAMS = pltpu.CompilerParams(vmem_limit_bytes=16 * 1024 * 1024)
NT = (((1,), (1,)), ((), ()))


def is_power(n):
    return n & (n - 1) == 0


def receiver(me, k, n):
    return me ^ k if is_power(n) else lax.rem(me + k, n)


def sender(me, k, n):
    return me ^ k if is_power(n) else lax.rem(me + n - k, n)


def survey_pairs(k, n):
    return [(i, i ^ k if is_power(n) else (i + k) % n) for i in range(n)]


def iota(shape, dim):
    return lax.broadcasted_iota(jnp.int32, shape, dim)


def time_of(sample, samples):
    return (sample.astype(f32) - (samples - 1) / 2.0) / (samples / 2.0)


def time_column(samples, lanes):
    return time_of(iota((samples, lanes), 0), samples)


def joined_blocks(data_ref, start):
    rows_x, rows_y = data_ref.shape[1:3]
    block = start // rows_y
    split = start - block * rows_y
    after = jnp.minimum(block + 1, rows_x - 1)
    here = data_ref[0, block].astype(f32)
    there = data_ref[0, after].astype(f32)
    return jnp.where(iota(here.shape, 0) >= split, here, there).astype(data_ref.dtype)


def first_of(index_ref, source, destination):
    return index_ref[source, 0, pl.ds(destination, 1), :][0, 0]


def pack_kernel(n, index_hbm, data_hbm, *refs):
    out_refs, (data_ref, index_ref, sems) = refs[: n - 1], refs[n - 1 :]
    index_copy = pltpu.make_async_copy(index_hbm, index_ref, sems.at[0])
    data_copy = pltpu.make_async_copy(data_hbm, data_ref, sems.at[1])
    index_copy.start()
    data_copy.start()
    me = lax.axis_index("survey")
    index_copy.wait()
    starts = [first_of(index_ref, me, receiver(me, k, n)) for k in range(1, n)]
    data_copy.wait()
    for out_ref, start in zip(out_refs, starts):
        out_ref[...] = joined_blocks(data_ref, start)


def put_rows(ref, k, rows):
    for i, row in enumerate(rows):
        ref[k, i : i + 1, :] = row


def mean_over(values):
    return jnp.sum(values, axis=0, keepdims=True) * (1.0 / values.shape[0])


def energy_rows(vals, moved, time_pos):
    tilted = time_pos * vals
    return [mean_over(moved * moved), mean_over(vals * vals), mean_over(tilted * tilted)]


def prepare_kernel(n, index_ref, count_ref, data_ref, basis_ref, own_ref, moved_ref, mask_ref, energy_ref, slope_ref):
    me = lax.axis_index("survey")
    samples, rows_y = own_ref.shape[1:]
    rows_x = data_ref.shape[1]
    row, col = iota((samples, samples), 0), iota((samples, samples), 1)
    basis_ref[:samples, :] = jnp.where(row == col, 1.0, 0.0).astype(bf16)
    basis_ref[samples:, :] = (jnp.where(col == row + 1, 0.5, 0.0) - jnp.where(col == row - 1, 0.5, 0.0)).astype(bf16)
    time_pos = time_column(samples, rows_y)
    position = iota((rows_x, rows_y), 0) * rows_y + iota((rows_x, rows_y), 1)
    for k in range(1, n):
        source = sender(me, k, n)
        start = first_of(index_ref, source, me)
        counts = count_ref[source]
        count = jnp.sum(jnp.where(iota(counts.shape, 1) == me, counts, 0))
        mask_ref[k - 1] = jnp.where((position >= start) & (position < start + count), 1.0, 0.0)
        rows = joined_blocks(data_ref, start)
        both = lax.dot_general(basis_ref[...], rows, NT, preferred_element_type=f32)
        own_ref[k - 1] = both[:samples]
        moved_ref[k - 1] = both[samples:]
        put_rows(energy_ref, k - 1, energy_rows(both[:samples], both[samples:], time_pos))
    for x in range(rows_x):
        block = slice(x * rows_y, (x + 1) * rows_y)
        slope_ref[block, :] = lax.dot_general(data_ref[0, x], basis_ref[samples:, :], NT, preferred_element_type=f32)


def corrected_lanes(values, moved, fields_ref, mask, time_pos):
    shift, gain, trend = [jnp.sum(fields_ref[c] * mask, axis=0, keepdims=True) for c in range(3)]
    amplitude = jnp.exp(gain + trend * time_pos)
    return (amplitude * (values + shift * moved)).astype(bf16)


def refresh_kernel(n, fields_ref, basis_ref, own_ref, moved_ref, mask_ref, *refs):
    arrived = refs[: n - 1]
    new_own_ref, new_moved_ref, energy_ref, partner_ref, partner_moved_ref = refs[n - 1 :]
    samples, rows_y = own_ref.shape[1:]
    time_pos = time_column(samples, rows_y)
    for k in range(n - 1):
        rounded = corrected_lanes(own_ref[k], moved_ref[k], fields_ref, mask_ref[k], time_pos)
        vals = rounded.astype(f32)
        moved = jnp.dot(basis_ref[samples:, :], rounded, preferred_element_type=f32)
        new_own_ref[k] = vals
        new_moved_ref[k] = moved
        put_rows(energy_ref, k, energy_rows(vals, moved, time_pos))
        both = lax.dot_general(basis_ref[...], arrived[k][...], NT, preferred_element_type=f32)
        partner_ref[k] = both[:samples]
        partner_moved_ref[k] = both[samples:]


def add_pair(sums, own, moved, partner, mask, energy_ref, k, time_pos):
    residual = partner - own
    along = residual * own
    slope_sum = mean_over(residual * moved)
    gain_sum = mean_over(along)
    trend_sum = mean_over(time_pos * along)
    cross_term = mean_over(own * partner)
    other_energy = mean_over(partner * partner)
    energy = [energy_ref[k, i : i + 1, :] for i in range(3)]
    weight = cross_term * cross_term / ((energy[1] + sim_eps) * (other_energy + sim_eps))
    for c, row in enumerate([slope_sum, gain_sum, trend_sum] + energy):
        term = mask * (weight * row)
        sums[c] = term if sums[c] is None else sums[c] + term


def pair_first_kernel(n, basis_ref, own_ref, moved_ref, mask_ref, energy_ref, *refs):
    arrived, out_ref = refs[: n - 1], refs[-1]
    samples, rows_y = own_ref.shape[1:]
    time_pos = time_column(samples, rows_y)
    sums = [None] * 6
    for k in range(n - 1):
        partner = lax.dot_general(basis_ref[:samples, :], arrived[k][...], NT, preferred_element_type=f32)
        add_pair(sums, own_ref[k], moved_ref[k], partner, mask_ref[k], energy_ref, k, time_pos)
    for c in range(6):
        out_ref[c] = sums[c]


def pair_next_kernel(n, own_ref, moved_ref, mask_ref, energy_ref, partner_ref, partner_moved_ref, *refs):
    field_refs, out_ref = refs[: n - 1], refs[-1]
    samples, rows_y = own_ref.shape[1:]
    time_pos = time_column(samples, rows_y)
    sums = [None] * 6
    for k in range(n - 1):
        partner = corrected_lanes(partner_ref[k], partner_moved_ref[k], field_refs[k], mask_ref[k], time_pos)
        add_pair(sums, own_ref[k], moved_ref[k], partner.astype(f32), mask_ref[k], energy_ref, k, time_pos)
    for c in range(6):
        out_ref[c] = sums[c]


def grid_solve(masks, smoothing_ref, piece_refs, grid_ref, tile):
    rows_x = piece_refs[0].shape[1]
    for piece, mask in zip(piece_refs, masks):
        spot = pl.multiple_of((tile ^ mask) * rows_x, rows_x)
        for c in range(6):
            grid_ref[c, pl.ds(spot, rows_x), :] = piece[c]
    size_x, size_y = grid_ref.shape[1:]
    grid_x = iota((size_x, size_y), 0)
    grid_y = iota((size_x, size_y), 1)
    each = range(3)

    def total(q):
        return jnp.sum(jnp.sum(q, axis=0, keepdims=True), axis=1, keepdims=True)

    def beside(v):
        return (
            jnp.where(grid_x > 0, pltpu.roll(v, 1, 0), 0.0)
            + jnp.where(grid_x < size_x - 1, pltpu.roll(v, size_x - 1, 0), 0.0)
            + jnp.where(grid_y > 0, pltpu.roll(v, 1, 1), 0.0)
            + jnp.where(grid_y < size_y - 1, pltpu.roll(v, size_y - 1, 1), 0.0)
        )

    strength = [smoothing_ref[0:1, c : c + 1] for c in each]
    diagonal = [grid_ref[3 + c] + (damping + 4.0 * strength[c]) for c in each]

    def apply(v):
        near = [beside(v[c]) for c in each]
        return [diagonal[c] * v[c] - strength[c] * near[c] for c in each]

    residual = [grid_ref[c] for c in each]
    image = apply(residual)
    norm_now = [total(residual[c] * residual[c]) for c in each]
    product = [total(residual[c] * image[c]) for c in each]
    alpha = [norm_now[c] / product[c] for c in each]
    direction, along = residual, image
    update = [alpha[c] * direction[c] for c in each]
    for iteration in range(1, CG_ITERS):
        residual = [residual[c] - alpha[c] * along[c] for c in each]
        image = apply(residual)
        norm_next = [total(residual[c] * residual[c]) for c in each]
        product = [total(residual[c] * image[c]) for c in each]
        ratio = [norm_next[c] / norm_now[c] for c in each]
        alpha = [norm_next[c] / (product[c] - ratio[c] * norm_next[c] / alpha[c]) for c in each]
        direction = [residual[c] + ratio[c] * direction[c] for c in each]
        if iteration + 1 < CG_ITERS:
            along = [image[c] + ratio[c] * along[c] for c in each]
        update = [update[c] + alpha[c] * direction[c] for c in each]
        norm_now = norm_next
    return update


def tile_part(grid_ref, c, tile, rows_x):
    return grid_ref[c, pl.ds(pl.multiple_of(tile * rows_x, rows_x), rows_x), :]


def solve_first_kernel(masks, smoothing_ref, *refs):
    pieces = refs[: len(masks)]
    fields_ref, beside_ref, grid_ref = refs[len(masks) :]
    tile = lax.axis_index("tile")
    updates = grid_solve(masks, smoothing_ref, pieces, grid_ref, tile)
    for c in range(3):
        grid_ref[c] = updates[c]
        fields_ref[c] = tile_part(grid_ref, c, tile, fields_ref.shape[1])
        beside_ref[c] = tile_part(grid_ref, c, tile ^ 1, fields_ref.shape[1])


def three_parts(values):
    parts = []
    for _ in range(3):
        part = values.astype(bf16).astype(f32)
        parts.append(part)
        values = values - part
    return parts


def solve_last_kernel(masks, smoothing_ref, before_ref, data_ref, slope_ref, *refs):
    pieces = refs[: len(masks)]
    fields_out, volume_ref, grid_ref, fields_ref, block_ref, sems = refs[len(masks) :]
    tile = lax.axis_index("tile")
    rows_x, rows_y = fields_ref.shape[1:]
    samples = data_ref.shape[3]
    lanes = 16 * rows_x
    kind = iota((lanes, samples), 0) // rows_x
    time_pos = time_of(iota((lanes, samples), 1), samples)
    spread_power = jnp.where((kind >= 3) & (kind < 6), 1.0, jnp.where((kind >= 6) & (kind < 9), time_pos, 0.0))
    spread_shift = jnp.where(kind[:, :rows_y] < 3, 1.0, 0.0)
    spread = jnp.concatenate([spread_shift, spread_power], axis=1).astype(bf16)
    which = lax.rem(iota((rows_y, lanes), 1), rows_x)
    updates = grid_solve(masks, smoothing_ref, pieces, grid_ref, tile)
    parts = []
    for c in range(3):
        grid_ref[c] = updates[c]
        mine = before_ref[c] + tile_part(grid_ref, c, tile, rows_x)
        fields_ref[c] = mine
        parts += three_parts(mine)
    copies = [pltpu.make_async_copy(fields_ref, fields_out, sems.at[rows_x])]
    copies[0].start()
    parts.append(jnp.zeros((lanes - 9 * rows_x, rows_y), f32))
    columns = jnp.transpose(jnp.concatenate(parts, axis=0))
    for x in range(rows_x):
        rows = slice(x * rows_y, (x + 1) * rows_y)
        mine = jnp.where(which == x, columns, 0.0).astype(bf16)
        both = jnp.dot(mine, spread, preferred_element_type=f32)
        shift = jnp.concatenate([both[:, :rows_y]] * (samples // rows_y), axis=1)
        moved = data_ref[0, x].astype(f32) + shift * slope_ref[rows, :]
        block_ref[rows, :] = (jnp.exp(both[:, rows_y:]) * moved).astype(volume_ref.dtype)
        copy = pltpu.make_async_copy(block_ref.at[rows, :], volume_ref.at[rows, :], sems.at[x])
        copy.start()
        copies.append(copy)
    for copy in copies:
        copy.wait()


def gather_tiles(piece, n):
    pieces = {0: piece}
    for mask in range(3, n, 2):
        pieces[mask] = lax.ppermute(piece, "tile", [(i, i ^ mask) for i in range(n)])
    if n > 1:
        for mask in list(pieces):
            pieces[mask ^ 1] = lax.ppermute(pieces[mask], "tile", [(i, i ^ 1) for i in range(n)])
    masks = sorted(pieces)
    return masks, [pieces[m] for m in masks]


def exchange(arrays, n):
    got = []
    for k in range(1, n):
        got.append(lax.ppermute(arrays[k - 1], "survey", survey_pairs(k, n)))
    return got


def exchange_across(array, n, n_tile):
    got = []
    for k in range(1, n):
        pairs = [(s * n_tile + t, d * n_tile + (t ^ 1)) for s, d in survey_pairs(k, n) for t in range(n_tile)]
        got.append(lax.ppermute(array, ("survey", "tile"), pairs))
    return got


def call(kernel, out_shape, n_in, **options):
    single = not isinstance(out_shape, list)
    options = {"out_specs": VMEM if single else [VMEM] * len(out_shape), "in_specs": [VMEM] * n_in, **options}
    return pl.pallas_call(kernel, out_shape=out_shape, compiler_params=PARAMS, **options)


def local(n_survey, n_tile, data, correlation_index, correlation_count, smoothing):
    rows_x, rows_y, samples = data.shape[1:]
    total, cap = rows_x * rows_y, correlation_index.shape[-1]
    assert cap <= rows_y and samples % rows_y == 0 and samples <= 256 and is_power(samples) and is_power(n_tile) and n_tile > 1
    others = n_survey - 1
    smoothing = smoothing.reshape(1, 3)
    packed = jax.ShapeDtypeStruct((rows_y, samples), data.dtype)
    field_shape = jax.ShapeDtypeStruct((3, rows_x, rows_y), f32)
    term_shape = jax.ShapeDtypeStruct((6, rows_x, rows_y), f32)
    lane_shape = jax.ShapeDtypeStruct((others, samples, rows_y), f32)
    mask_shape = jax.ShapeDtypeStruct((others, rows_x, rows_y), f32)
    energy_shape = jax.ShapeDtypeStruct((others, 8, rows_y), f32)
    basis_shape = jax.ShapeDtypeStruct((2 * samples, samples), bf16)
    slope_shape = jax.ShapeDtypeStruct((total, samples), f32)
    volume_shape = jax.ShapeDtypeStruct((total, samples), data.dtype)
    grid = pltpu.VMEM((6, rows_x * n_tile, rows_y), f32)

    *outgoing, data = call(
        functools.partial(pack_kernel, n_survey),
        [packed] * others + [jax.ShapeDtypeStruct(data.shape, data.dtype)],
        2,
        in_specs=[HBM] * 2,
        scratch_shapes=[pltpu.VMEM(correlation_index.shape, jnp.int32), pltpu.SemaphoreType.DMA((2,))],
    )(*[pltpu.with_memory_space_constraint(a, pltpu.HBM) for a in (correlation_index, data)])
    arrived = exchange(outgoing, n_survey)
    basis, own, moved, mask, energy, slope = call(
        functools.partial(prepare_kernel, n_survey),
        [basis_shape, lane_shape, lane_shape, mask_shape, energy_shape, slope_shape],
        3,
    )(correlation_index, correlation_count, data)
    terms = call(functools.partial(pair_first_kernel, n_survey), term_shape, 5 + others)(
        basis, own, moved, mask, energy, *arrived
    )
    masks, pieces = gather_tiles(terms, n_tile)
    fields, beside = call(
        functools.partial(solve_first_kernel, masks), [field_shape] * 2, 1 + n_tile, scratch_shapes=[grid]
    )(smoothing, *pieces)

    partner_fields = exchange_across(beside, n_survey, n_tile)
    own, moved, energy, partner, partner_moved = call(
        functools.partial(refresh_kernel, n_survey),
        [lane_shape, lane_shape, energy_shape, lane_shape, lane_shape],
        5 + others,
    )(fields, basis, own, moved, mask, *arrived)
    terms = call(functools.partial(pair_next_kernel, n_survey), term_shape, 6 + others)(
        own, moved, mask, energy, partner, partner_moved, *partner_fields
    )
    masks, pieces = gather_tiles(terms, n_tile)
    fields, volume = call(
        functools.partial(solve_last_kernel, masks),
        [field_shape, volume_shape],
        4 + n_tile,
        out_specs=[ANY, ANY],
        scratch_shapes=[
            grid,
            pltpu.VMEM((3, rows_x, rows_y), f32),
            pltpu.VMEM((total, samples), data.dtype),
            pltpu.SemaphoreType.DMA((rows_x + 1,)),
        ],
    )(smoothing, fields, data, slope, *pieces)
    return fields.reshape(1, 3, rows_x, rows_y), volume.reshape(1, rows_x, rows_y, samples)


def solution(mesh):
    placed = (
        P("survey", "tile", None, None),
        P(None, "tile", None, None),
        P(None, "tile", None),
        P(),
    )
    return jax.shard_map(
        functools.partial(local, mesh.shape["survey"], mesh.shape["tile"]),
        mesh=mesh,
        in_specs=placed,
        out_specs=(P("survey", None, "tile", None), P("survey", "tile", None, None)),
        check_vma=False,
    )
```

```python
import functools

import jax
import jax.numpy as jnp
from jax import lax
from jax.experimental import pallas as pl
from jax.experimental.pallas import tpu as pltpu
from jax.sharding import PartitionSpec as P


CG_ITERS = 3

damping = 0.05
sim_eps = 1e-05

f32 = jnp.float32
bf16 = jnp.bfloat16
VMEM = pl.BlockSpec(memory_space=pltpu.VMEM)
ANY = pl.BlockSpec(memory_space=pl.ANY)
HBM = pl.BlockSpec(memory_space=pltpu.HBM)
PARAMS = pltpu.CompilerParams(vmem_limit_bytes=16 * 1024 * 1024)
NT = (((1,), (1,)), ((), ()))


def is_power(n):
    return n & (n - 1) == 0


def receiver(me, k, n):
    return me ^ k if is_power(n) else lax.rem(me + k, n)


def sender(me, k, n):
    return me ^ k if is_power(n) else lax.rem(me + n - k, n)


def survey_pairs(k, n):
    return [(i, i ^ k if is_power(n) else (i + k) % n) for i in range(n)]


def iota(shape, dim):
    return lax.broadcasted_iota(jnp.int32, shape, dim)


def time_of(sample, samples):
    return (sample.astype(f32) - (samples - 1) / 2.0) / (samples / 2.0)


def time_column(samples, lanes):
    return time_of(iota((samples, lanes), 0), samples)


def joined_blocks(data_ref, start):
    rows_x, rows_y = data_ref.shape[1:3]
    block = start // rows_y
    split = start - block * rows_y
    after = jnp.minimum(block + 1, rows_x - 1)
    here = data_ref[0, block].astype(f32)
    there = data_ref[0, after].astype(f32)
    return jnp.where(iota(here.shape, 0) >= split, here, there).astype(data_ref.dtype)


def first_of(index_ref, source, destination):
    return index_ref[source, 0, pl.ds(destination, 1), :][0, 0]


def pack_kernel(n, index_hbm, data_hbm, *refs):
    out_refs, (data_ref, index_ref, sems) = refs[: n - 1], refs[n - 1 :]
    index_copy = pltpu.make_async_copy(index_hbm, index_ref, sems.at[0])
    data_copy = pltpu.make_async_copy(data_hbm, data_ref, sems.at[1])
    index_copy.start()
    data_copy.start()
    me = lax.axis_index("survey")
    index_copy.wait()
    starts = [first_of(index_ref, me, receiver(me, k, n)) for k in range(1, n)]
    data_copy.wait()
    for out_ref, start in zip(out_refs, starts):
        out_ref[...] = joined_blocks(data_ref, start)


def put_rows(ref, k, rows):
    for i, row in enumerate(rows):
        ref[k, i : i + 1, :] = row


def mean_over(values):
    return jnp.sum(values, axis=0, keepdims=True) * (1.0 / values.shape[0])


def energy_rows(vals, moved, time_pos):
    tilted = time_pos * vals
    return [mean_over(moved * moved), mean_over(vals * vals), mean_over(tilted * tilted)]


def prepare_kernel(n, index_ref, count_ref, data_ref, basis_ref, own_ref, moved_ref, mask_ref, energy_ref, slope_ref):
    me = lax.axis_index("survey")
    samples, rows_y = own_ref.shape[1:]
    rows_x = data_ref.shape[1]
    row, col = iota((samples, samples), 0), iota((samples, samples), 1)
    basis_ref[:samples, :] = jnp.where(row == col, 1.0, 0.0).astype(bf16)
    basis_ref[samples:, :] = (jnp.where(col == row + 1, 0.5, 0.0) - jnp.where(col == row - 1, 0.5, 0.0)).astype(bf16)
    time_pos = time_column(samples, rows_y)
    position = iota((rows_x, rows_y), 0) * rows_y + iota((rows_x, rows_y), 1)
    for k in range(1, n):
        source = sender(me, k, n)
        start = first_of(index_ref, source, me)
        counts = count_ref[source]
        count = jnp.sum(jnp.where(iota(counts.shape, 1) == me, counts, 0))
        mask_ref[k - 1] = jnp.where((position >= start) & (position < start + count), 1.0, 0.0)
        rows = joined_blocks(data_ref, start)
        both = lax.dot_general(basis_ref[...], rows, NT, preferred_element_type=f32)
        own_ref[k - 1] = both[:samples]
        moved_ref[k - 1] = both[samples:]
        put_rows(energy_ref, k - 1, energy_rows(both[:samples], both[samples:], time_pos))
    for x in range(rows_x):
        block = slice(x * rows_y, (x + 1) * rows_y)
        slope_ref[block, :] = lax.dot_general(data_ref[0, x], basis_ref[samples:, :], NT, preferred_element_type=f32)


def corrected_lanes(values, moved, fields_ref, mask, time_pos):
    shift, gain, trend = [jnp.sum(fields_ref[c] * mask, axis=0, keepdims=True) for c in range(3)]
    amplitude = jnp.exp(gain + trend * time_pos)
    return (amplitude * (values + shift * moved)).astype(bf16)


def refresh_kernel(n, fields_ref, basis_ref, own_ref, moved_ref, mask_ref, *refs):
    arrived = refs[: n - 1]
    new_own_ref, new_moved_ref, energy_ref, partner_ref, partner_moved_ref = refs[n - 1 :]
    samples, rows_y = own_ref.shape[1:]
    time_pos = time_column(samples, rows_y)
    for k in range(n - 1):
        rounded = corrected_lanes(own_ref[k], moved_ref[k], fields_ref, mask_ref[k], time_pos)
        vals = rounded.astype(f32)
        moved = jnp.dot(basis_ref[samples:, :], rounded, preferred_element_type=f32)
        new_own_ref[k] = vals
        new_moved_ref[k] = moved
        put_rows(energy_ref, k, energy_rows(vals, moved, time_pos))
        both = lax.dot_general(basis_ref[...], arrived[k][...], NT, preferred_element_type=f32)
        partner_ref[k] = both[:samples]
        partner_moved_ref[k] = both[samples:]


def add_pair(sums, own, moved, partner, mask, energy_ref, k, time_pos):
    residual = partner - own
    along = residual * own
    slope_sum = mean_over(residual * moved)
    gain_sum = mean_over(along)
    trend_sum = mean_over(time_pos * along)
    cross_term = mean_over(own * partner)
    other_energy = mean_over(partner * partner)
    energy = [energy_ref[k, i : i + 1, :] for i in range(3)]
    weight = cross_term * cross_term / ((energy[1] + sim_eps) * (other_energy + sim_eps))
    for c, row in enumerate([slope_sum, gain_sum, trend_sum] + energy):
        term = mask * (weight * row)
        sums[c] = term if sums[c] is None else sums[c] + term


def pair_first_kernel(n, basis_ref, own_ref, moved_ref, mask_ref, energy_ref, *refs):
    arrived, out_ref = refs[: n - 1], refs[-1]
    samples, rows_y = own_ref.shape[1:]
    time_pos = time_column(samples, rows_y)
    sums = [None] * 6
    for k in range(n - 1):
        partner = lax.dot_general(basis_ref[:samples, :], arrived[k][...], NT, preferred_element_type=f32)
        add_pair(sums, own_ref[k], moved_ref[k], partner, mask_ref[k], energy_ref, k, time_pos)
    for c in range(6):
        out_ref[c] = sums[c]


def pair_next_kernel(n, own_ref, moved_ref, mask_ref, energy_ref, partner_ref, partner_moved_ref, *refs):
    field_refs, out_ref = refs[: n - 1], refs[-1]
    samples, rows_y = own_ref.shape[1:]
    time_pos = time_column(samples, rows_y)
    sums = [None] * 6
    for k in range(n - 1):
        partner = corrected_lanes(partner_ref[k], partner_moved_ref[k], field_refs[k], mask_ref[k], time_pos)
        add_pair(sums, own_ref[k], moved_ref[k], partner.astype(f32), mask_ref[k], energy_ref, k, time_pos)
    for c in range(6):
        out_ref[c] = sums[c]


def grid_solve(masks, smoothing_ref, piece_refs, grid_ref, tile):
    rows_x = piece_refs[0].shape[1]
    for piece, mask in zip(piece_refs, masks):
        spot = pl.multiple_of((tile ^ mask) * rows_x, rows_x)
        for c in range(6):
            grid_ref[c, pl.ds(spot, rows_x), :] = piece[c]
    size_x, size_y = grid_ref.shape[1:]
    grid_x = iota((size_x, size_y), 0)
    grid_y = iota((size_x, size_y), 1)
    each = range(3)

    def total(q):
        return jnp.sum(jnp.sum(q, axis=0, keepdims=True), axis=1, keepdims=True)

    def beside(v):
        return (
            jnp.where(grid_x > 0, pltpu.roll(v, 1, 0), 0.0)
            + jnp.where(grid_x < size_x - 1, pltpu.roll(v, size_x - 1, 0), 0.0)
            + jnp.where(grid_y > 0, pltpu.roll(v, 1, 1), 0.0)
            + jnp.where(grid_y < size_y - 1, pltpu.roll(v, size_y - 1, 1), 0.0)
        )

    strength = [smoothing_ref[0:1, c : c + 1] for c in each]
    diagonal = [grid_ref[3 + c] + (damping + 4.0 * strength[c]) for c in each]

    def apply(v):
        near = [beside(v[c]) for c in each]
        return [diagonal[c] * v[c] - strength[c] * near[c] for c in each]

    residual = [grid_ref[c] for c in each]
    image = apply(residual)
    norm_before, alpha = [None] * 3, [None] * 3
    direction, along, beyond, update = [None] * 3, [None] * 3, [None] * 3, [None] * 3
    for iteration in range(CG_ITERS):
        last = iteration + 1 == CG_ITERS
        norm_now = [total(residual[c] * residual[c]) for c in each]
        product = [total(residual[c] * image[c]) for c in each]
        further = None if last else apply(image)
        for c in each:
            if iteration == 0:
                alpha[c] = norm_now[c] / product[c]
                direction[c], along[c] = residual[c], image[c]
                beyond[c] = None if last else further[c]
                update[c] = alpha[c] * direction[c]
            else:
                ratio = norm_now[c] / norm_before[c]
                alpha[c] = norm_now[c] / (product[c] - ratio * norm_now[c] / alpha[c])
                direction[c] = residual[c] + ratio * direction[c]
                if not last:
                    along[c] = image[c] + ratio * along[c]
                    beyond[c] = further[c] + ratio * beyond[c]
                update[c] = update[c] + alpha[c] * direction[c]
            if not last:
                residual[c] = residual[c] - alpha[c] * along[c]
                image[c] = image[c] - alpha[c] * beyond[c]
        norm_before = norm_now
    return update


def tile_part(grid_ref, c, tile, rows_x):
    return grid_ref[c, pl.ds(pl.multiple_of(tile * rows_x, rows_x), rows_x), :]


def solve_first_kernel(masks, smoothing_ref, *refs):
    pieces = refs[: len(masks)]
    fields_ref, beside_ref, grid_ref = refs[len(masks) :]
    tile = lax.axis_index("tile")
    updates = grid_solve(masks, smoothing_ref, pieces, grid_ref, tile)
    for c in range(3):
        grid_ref[c] = updates[c]
        fields_ref[c] = tile_part(grid_ref, c, tile, fields_ref.shape[1])
        beside_ref[c] = tile_part(grid_ref, c, tile ^ 1, fields_ref.shape[1])


def three_parts(values):
    parts = []
    for _ in range(3):
        part = values.astype(bf16).astype(f32)
        parts.append(part)
        values = values - part
    return parts


def solve_last_kernel(masks, smoothing_ref, before_ref, data_ref, slope_ref, *refs):
    pieces = refs[: len(masks)]
    fields_out, volume_ref, grid_ref, fields_ref, block_ref, sems = refs[len(masks) :]
    tile = lax.axis_index("tile")
    rows_x, rows_y = fields_ref.shape[1:]
    samples = data_ref.shape[3]
    lanes = 16 * rows_x
    kind = iota((lanes, samples), 0) // rows_x
    time_pos = time_of(iota((lanes, samples), 1), samples)
    spread_power = jnp.where((kind >= 3) & (kind < 6), 1.0, jnp.where((kind >= 6) & (kind < 9), time_pos, 0.0))
    spread_shift = jnp.where(kind[:, :rows_y] < 3, 1.0, 0.0)
    spread = jnp.concatenate([spread_shift, spread_power], axis=1).astype(bf16)
    which = lax.rem(iota((rows_y, lanes), 1), rows_x)
    updates = grid_solve(masks, smoothing_ref, pieces, grid_ref, tile)
    parts = []
    for c in range(3):
        grid_ref[c] = updates[c]
        mine = before_ref[c] + tile_part(grid_ref, c, tile, rows_x)
        fields_ref[c] = mine
        parts += three_parts(mine)
    copies = [pltpu.make_async_copy(fields_ref, fields_out, sems.at[rows_x])]
    copies[0].start()
    parts.append(jnp.zeros((lanes - 9 * rows_x, rows_y), f32))
    columns = jnp.transpose(jnp.concatenate(parts, axis=0))
    for x in range(rows_x):
        rows = slice(x * rows_y, (x + 1) * rows_y)
        mine = jnp.where(which == x, columns, 0.0).astype(bf16)
        both = jnp.dot(mine, spread, preferred_element_type=f32)
        shift = jnp.concatenate([both[:, :rows_y]] * (samples // rows_y), axis=1)
        moved = data_ref[0, x].astype(f32) + shift * slope_ref[rows, :]
        block_ref[rows, :] = (jnp.exp(both[:, rows_y:]) * moved).astype(volume_ref.dtype)
        copy = pltpu.make_async_copy(block_ref.at[rows, :], volume_ref.at[rows, :], sems.at[x])
        copy.start()
        copies.append(copy)
    for copy in copies:
        copy.wait()


def gather_tiles(piece, n):
    pieces = {0: piece}
    for mask in range(3, n, 2):
        pieces[mask] = lax.ppermute(piece, "tile", [(i, i ^ mask) for i in range(n)])
    if n > 1:
        for mask in list(pieces):
            pieces[mask ^ 1] = lax.ppermute(pieces[mask], "tile", [(i, i ^ 1) for i in range(n)])
    masks = sorted(pieces)
    return masks, [pieces[m] for m in masks]


def exchange(arrays, n):
    got = []
    for k in range(1, n):
        got.append(lax.ppermute(arrays[k - 1], "survey", survey_pairs(k, n)))
    return got


def exchange_across(array, n, n_tile):
    got = []
    for k in range(1, n):
        pairs = [(s * n_tile + t, d * n_tile + (t ^ 1)) for s, d in survey_pairs(k, n) for t in range(n_tile)]
        got.append(lax.ppermute(array, ("survey", "tile"), pairs))
    return got


def call(kernel, out_shape, n_in, **options):
    single = not isinstance(out_shape, list)
    options = {"out_specs": VMEM if single else [VMEM] * len(out_shape), "in_specs": [VMEM] * n_in, **options}
    return pl.pallas_call(kernel, out_shape=out_shape, compiler_params=PARAMS, **options)


def local(n_survey, n_tile, data, correlation_index, correlation_count, smoothing):
    rows_x, rows_y, samples = data.shape[1:]
    total, cap = rows_x * rows_y, correlation_index.shape[-1]
    assert cap <= rows_y and samples % rows_y == 0 and samples <= 256 and is_power(samples) and is_power(n_tile) and n_tile > 1
    others = n_survey - 1
    smoothing = smoothing.reshape(1, 3)
    packed = jax.ShapeDtypeStruct((rows_y, samples), data.dtype)
    field_shape = jax.ShapeDtypeStruct((3, rows_x, rows_y), f32)
    term_shape = jax.ShapeDtypeStruct((6, rows_x, rows_y), f32)
    lane_shape = jax.ShapeDtypeStruct((others, samples, rows_y), f32)
    mask_shape = jax.ShapeDtypeStruct((others, rows_x, rows_y), f32)
    energy_shape = jax.ShapeDtypeStruct((others, 8, rows_y), f32)
    basis_shape = jax.ShapeDtypeStruct((2 * samples, samples), bf16)
    slope_shape = jax.ShapeDtypeStruct((total, samples), f32)
    volume_shape = jax.ShapeDtypeStruct((total, samples), data.dtype)
    grid = pltpu.VMEM((6, rows_x * n_tile, rows_y), f32)

    *outgoing, data = call(
        functools.partial(pack_kernel, n_survey),
        [packed] * others + [jax.ShapeDtypeStruct(data.shape, data.dtype)],
        2,
        in_specs=[HBM] * 2,
        scratch_shapes=[pltpu.VMEM(correlation_index.shape, jnp.int32), pltpu.SemaphoreType.DMA((2,))],
    )(*[pltpu.with_memory_space_constraint(a, pltpu.HBM) for a in (correlation_index, data)])
    arrived = exchange(outgoing, n_survey)
    basis, own, moved, mask, energy, slope = call(
        functools.partial(prepare_kernel, n_survey),
        [basis_shape, lane_shape, lane_shape, mask_shape, energy_shape, slope_shape],
        3,
    )(correlation_index, correlation_count, data)
    terms = call(functools.partial(pair_first_kernel, n_survey), term_shape, 5 + others)(
        basis, own, moved, mask, energy, *arrived
    )
    masks, pieces = gather_tiles(terms, n_tile)
    fields, beside = call(
        functools.partial(solve_first_kernel, masks), [field_shape] * 2, 1 + n_tile, scratch_shapes=[grid]
    )(smoothing, *pieces)

    partner_fields = exchange_across(beside, n_survey, n_tile)
    own, moved, energy, partner, partner_moved = call(
        functools.partial(refresh_kernel, n_survey),
        [lane_shape, lane_shape, energy_shape, lane_shape, lane_shape],
        5 + others,
    )(fields, basis, own, moved, mask, *arrived)
    terms = call(functools.partial(pair_next_kernel, n_survey), term_shape, 6 + others)(
        own, moved, mask, energy, partner, partner_moved, *partner_fields
    )
    masks, pieces = gather_tiles(terms, n_tile)
    fields, volume = call(
        functools.partial(solve_last_kernel, masks),
        [field_shape, volume_shape],
        4 + n_tile,
        out_specs=[ANY, ANY],
        scratch_shapes=[
            grid,
            pltpu.VMEM((3, rows_x, rows_y), f32),
            pltpu.VMEM((total, samples), data.dtype),
            pltpu.SemaphoreType.DMA((rows_x + 1,)),
        ],
    )(smoothing, fields, data, slope, *pieces)
    return fields.reshape(1, 3, rows_x, rows_y), volume.reshape(1, rows_x, rows_y, samples)


def solution(mesh):
    placed = (
        P("survey", "tile", None, None),
        P(None, "tile", None, None),
        P(None, "tile", None),
        P(),
    )
    return jax.shard_map(
        functools.partial(local, mesh.shape["survey"], mesh.shape["tile"]),
        mesh=mesh,
        in_specs=placed,
        out_specs=(P("survey", None, "tile", None), P("survey", "tile", None, None)),
        check_vma=False,
    )
```

```python
import functools

import jax
import jax.numpy as jnp
from jax import lax
from jax.experimental import pallas as pl
from jax.experimental.pallas import tpu as pltpu
from jax.sharding import PartitionSpec as P


CG_ITERS = 3

damping = 0.05
sim_eps = 1e-05

f32 = jnp.float32
bf16 = jnp.bfloat16
VMEM = pl.BlockSpec(memory_space=pltpu.VMEM)
ANY = pl.BlockSpec(memory_space=pl.ANY)
HBM = pl.BlockSpec(memory_space=pltpu.HBM)
PARAMS = pltpu.CompilerParams(vmem_limit_bytes=16 * 1024 * 1024)
NT = (((1,), (1,)), ((), ()))


def is_power(n):
    return n & (n - 1) == 0


def receiver(me, k, n):
    return me ^ k if is_power(n) else lax.rem(me + k, n)


def sender(me, k, n):
    return me ^ k if is_power(n) else lax.rem(me + n - k, n)


def survey_pairs(k, n):
    return [(i, i ^ k if is_power(n) else (i + k) % n) for i in range(n)]


def iota(shape, dim):
    return lax.broadcasted_iota(jnp.int32, shape, dim)


def time_of(sample, samples):
    return (sample.astype(f32) - (samples - 1) / 2.0) / (samples / 2.0)


def time_column(samples, lanes):
    return time_of(iota((samples, lanes), 0), samples)


def joined_blocks(data_ref, start):
    rows_x, rows_y = data_ref.shape[1:3]
    block = start // rows_y
    split = start - block * rows_y
    after = jnp.minimum(block + 1, rows_x - 1)
    here = data_ref[0, block].astype(f32)
    there = data_ref[0, after].astype(f32)
    return jnp.where(iota(here.shape, 0) >= split, here, there).astype(data_ref.dtype)


def first_of(index_ref, source, destination):
    return index_ref[source, 0, pl.ds(destination, 1), :][0, 0]


def pack_kernel(n, index_hbm, data_hbm, *refs):
    out_refs, (data_ref, index_ref, sems) = refs[: n - 1], refs[n - 1 :]
    index_copy = pltpu.make_async_copy(index_hbm, index_ref, sems.at[0])
    data_copy = pltpu.make_async_copy(data_hbm, data_ref, sems.at[1])
    index_copy.start()
    data_copy.start()
    me = lax.axis_index("survey")
    index_copy.wait()
    starts = [first_of(index_ref, me, receiver(me, k, n)) for k in range(1, n)]
    data_copy.wait()
    for out_ref, start in zip(out_refs, starts):
        out_ref[...] = joined_blocks(data_ref, start)


def put_rows(ref, k, rows):
    for i, row in enumerate(rows):
        ref[k, i : i + 1, :] = row


def mean_over(values):
    return jnp.sum(values, axis=0, keepdims=True) * (1.0 / values.shape[0])


def energy_rows(vals, moved, time_pos):
    tilted = time_pos * vals
    return [mean_over(moved * moved), mean_over(vals * vals), mean_over(tilted * tilted)]


def prepare_kernel(n, index_ref, count_ref, data_ref, basis_ref, own_ref, moved_ref, mask_ref, energy_ref, slope_ref):
    me = lax.axis_index("survey")
    samples, rows_y = own_ref.shape[1:]
    rows_x = data_ref.shape[1]
    row, col = iota((samples, samples), 0), iota((samples, samples), 1)
    basis_ref[:samples, :] = jnp.where(row == col, 1.0, 0.0).astype(bf16)
    basis_ref[samples:, :] = (jnp.where(col == row + 1, 0.5, 0.0) - jnp.where(col == row - 1, 0.5, 0.0)).astype(bf16)
    time_pos = time_column(samples, rows_y)
    position = iota((rows_x, rows_y), 0) * rows_y + iota((rows_x, rows_y), 1)
    for k in range(1, n):
        source = sender(me, k, n)
        start = first_of(index_ref, source, me)
        counts = count_ref[source]
        count = jnp.sum(jnp.where(iota(counts.shape, 1) == me, counts, 0))
        mask_ref[k - 1] = jnp.where((position >= start) & (position < start + count), 1.0, 0.0)
        rows = joined_blocks(data_ref, start)
        both = lax.dot_general(basis_ref[...], rows, NT, preferred_element_type=f32)
        own_ref[k - 1] = both[:samples]
        moved_ref[k - 1] = both[samples:]
        put_rows(energy_ref, k - 1, energy_rows(both[:samples], both[samples:], time_pos))
    for x in range(rows_x):
        block = slice(x * rows_y, (x + 1) * rows_y)
        slope_ref[block, :] = lax.dot_general(data_ref[0, x], basis_ref[samples:, :], NT, preferred_element_type=f32)


def corrected_lanes(values, moved, fields_ref, mask, time_pos):
    shift, gain, trend = [jnp.sum(fields_ref[c] * mask, axis=0, keepdims=True) for c in range(3)]
    amplitude = jnp.exp(gain + trend * time_pos)
    return (amplitude * (values + shift * moved)).astype(bf16)


def refresh_kernel(n, fields_ref, basis_ref, own_ref, moved_ref, mask_ref, *refs):
    arrived = refs[: n - 1]
    new_own_ref, new_moved_ref, energy_ref, partner_ref, partner_moved_ref = refs[n - 1 :]
    samples, rows_y = own_ref.shape[1:]
    time_pos = time_column(samples, rows_y)
    for k in range(n - 1):
        rounded = corrected_lanes(own_ref[k], moved_ref[k], fields_ref, mask_ref[k], time_pos)
        vals = rounded.astype(f32)
        moved = jnp.dot(basis_ref[samples:, :], rounded, preferred_element_type=f32)
        new_own_ref[k] = vals
        new_moved_ref[k] = moved
        put_rows(energy_ref, k, energy_rows(vals, moved, time_pos))
        both = lax.dot_general(basis_ref[...], arrived[k][...], NT, preferred_element_type=f32)
        partner_ref[k] = both[:samples]
        partner_moved_ref[k] = both[samples:]


def add_pair(sums, own, moved, partner, mask, energy_ref, k, time_pos):
    residual = partner - own
    along = residual * own
    slope_sum = mean_over(residual * moved)
    gain_sum = mean_over(along)
    trend_sum = mean_over(time_pos * along)
    cross_term = mean_over(own * partner)
    other_energy = mean_over(partner * partner)
    energy = [energy_ref[k, i : i + 1, :] for i in range(3)]
    weight = cross_term * cross_term / ((energy[1] + sim_eps) * (other_energy + sim_eps))
    for c, row in enumerate([slope_sum, gain_sum, trend_sum] + energy):
        term = mask * (weight * row)
        sums[c] = term if sums[c] is None else sums[c] + term


def pair_first_kernel(slots, basis_ref, own_ref, moved_ref, mask_ref, energy_ref, *refs):
    arrived, before, out_ref = refs[: len(slots)], refs[len(slots) : -1], refs[-1]
    samples, rows_y = own_ref.shape[1:]
    time_pos = time_column(samples, rows_y)
    sums = [before[0][c] if before else None for c in range(6)]
    for k, traces_ref in zip(slots, arrived):
        partner = lax.dot_general(basis_ref[:samples, :], traces_ref[...], NT, preferred_element_type=f32)
        add_pair(sums, own_ref[k], moved_ref[k], partner, mask_ref[k], energy_ref, k, time_pos)
    for c in range(6):
        out_ref[c] = sums[c]


def pair_next_kernel(n, own_ref, moved_ref, mask_ref, energy_ref, partner_ref, partner_moved_ref, *refs):
    field_refs, out_ref = refs[: n - 1], refs[-1]
    samples, rows_y = own_ref.shape[1:]
    time_pos = time_column(samples, rows_y)
    sums = [None] * 6
    for k in range(n - 1):
        partner = corrected_lanes(partner_ref[k], partner_moved_ref[k], field_refs[k], mask_ref[k], time_pos)
        add_pair(sums, own_ref[k], moved_ref[k], partner.astype(f32), mask_ref[k], energy_ref, k, time_pos)
    for c in range(6):
        out_ref[c] = sums[c]


def grid_solve(masks, smoothing_ref, piece_refs, grid_ref, tile):
    rows_x = piece_refs[0].shape[1]
    for piece, mask in zip(piece_refs, masks):
        spot = pl.multiple_of((tile ^ mask) * rows_x, rows_x)
        for c in range(6):
            grid_ref[c, pl.ds(spot, rows_x), :] = piece[c]
    size_x, size_y = grid_ref.shape[1:]
    grid_x = iota((size_x, size_y), 0)
    grid_y = iota((size_x, size_y), 1)
    each = range(3)

    def total(q):
        return jnp.sum(jnp.sum(q, axis=0, keepdims=True), axis=1, keepdims=True)

    def beside(v):
        return (
            jnp.where(grid_x > 0, pltpu.roll(v, 1, 0), 0.0)
            + jnp.where(grid_x < size_x - 1, pltpu.roll(v, size_x - 1, 0), 0.0)
            + jnp.where(grid_y > 0, pltpu.roll(v, 1, 1), 0.0)
            + jnp.where(grid_y < size_y - 1, pltpu.roll(v, size_y - 1, 1), 0.0)
        )

    strength = [smoothing_ref[0:1, c : c + 1] for c in each]
    diagonal = [grid_ref[3 + c] + (damping + 4.0 * strength[c]) for c in each]

    def apply(v):
        near = [beside(v[c]) for c in each]
        return [diagonal[c] * v[c] - strength[c] * near[c] for c in each]

    residual = [grid_ref[c] for c in each]
    image = apply(residual)
    norm_before, alpha = [None] * 3, [None] * 3
    direction, along, beyond, update = [None] * 3, [None] * 3, [None] * 3, [None] * 3
    for iteration in range(CG_ITERS):
        last = iteration + 1 == CG_ITERS
        norm_now = [total(residual[c] * residual[c]) for c in each]
        product = [total(residual[c] * image[c]) for c in each]
        further = None if last else apply(image)
        for c in each:
            if iteration == 0:
                alpha[c] = norm_now[c] / product[c]
                direction[c], along[c] = residual[c], image[c]
                beyond[c] = None if last else further[c]
                update[c] = alpha[c] * direction[c]
            else:
                ratio = norm_now[c] / norm_before[c]
                alpha[c] = norm_now[c] / (product[c] - ratio * norm_now[c] / alpha[c])
                direction[c] = residual[c] + ratio * direction[c]
                if not last:
                    along[c] = image[c] + ratio * along[c]
                    beyond[c] = further[c] + ratio * beyond[c]
                update[c] = update[c] + alpha[c] * direction[c]
            if not last:
                residual[c] = residual[c] - alpha[c] * along[c]
                image[c] = image[c] - alpha[c] * beyond[c]
        norm_before = norm_now
    return update


def tile_part(grid_ref, c, tile, rows_x):
    return grid_ref[c, pl.ds(pl.multiple_of(tile * rows_x, rows_x), rows_x), :]


def solve_first_kernel(masks, smoothing_ref, *refs):
    pieces = refs[: len(masks)]
    fields_ref, beside_ref, grid_ref = refs[len(masks) :]
    tile = lax.axis_index("tile")
    updates = grid_solve(masks, smoothing_ref, pieces, grid_ref, tile)
    for c in range(3):
        grid_ref[c] = updates[c]
        fields_ref[c] = tile_part(grid_ref, c, tile, fields_ref.shape[1])
        beside_ref[c] = tile_part(grid_ref, c, tile ^ 1, fields_ref.shape[1])


def three_parts(values):
    parts = []
    for _ in range(3):
        part = values.astype(bf16).astype(f32)
        parts.append(part)
        values = values - part
    return parts


def solve_last_kernel(masks, smoothing_ref, before_ref, data_ref, slope_ref, *refs):
    pieces = refs[: len(masks)]
    fields_out, volume_ref, grid_ref, fields_ref, block_ref, sems = refs[len(masks) :]
    tile = lax.axis_index("tile")
    rows_x, rows_y = fields_ref.shape[1:]
    samples = data_ref.shape[3]
    lanes = 16 * rows_x
    kind = iota((lanes, samples), 0) // rows_x
    time_pos = time_of(iota((lanes, samples), 1), samples)
    spread_power = jnp.where((kind >= 3) & (kind < 6), 1.0, jnp.where((kind >= 6) & (kind < 9), time_pos, 0.0))
    spread_shift = jnp.where(kind[:, :rows_y] < 3, 1.0, 0.0)
    spread = jnp.concatenate([spread_shift, spread_power], axis=1).astype(bf16)
    which = lax.rem(iota((rows_y, lanes), 1), rows_x)
    updates = grid_solve(masks, smoothing_ref, pieces, grid_ref, tile)
    parts = []
    for c in range(3):
        grid_ref[c] = updates[c]
        mine = before_ref[c] + tile_part(grid_ref, c, tile, rows_x)
        fields_ref[c] = mine
        parts += three_parts(mine)
    copies = [pltpu.make_async_copy(fields_ref, fields_out, sems.at[rows_x])]
    copies[0].start()
    parts.append(jnp.zeros((lanes - 9 * rows_x, rows_y), f32))
    columns = jnp.transpose(jnp.concatenate(parts, axis=0))
    for x in range(rows_x):
        rows = slice(x * rows_y, (x + 1) * rows_y)
        mine = jnp.where(which == x, columns, 0.0).astype(bf16)
        both = jnp.dot(mine, spread, preferred_element_type=f32)
        shift = jnp.concatenate([both[:, :rows_y]] * (samples // rows_y), axis=1)
        moved = data_ref[0, x].astype(f32) + shift * slope_ref[rows, :]
        block_ref[rows, :] = (jnp.exp(both[:, rows_y:]) * moved).astype(volume_ref.dtype)
        copy = pltpu.make_async_copy(block_ref.at[rows, :], volume_ref.at[rows, :], sems.at[x])
        copy.start()
        copies.append(copy)
    for copy in copies:
        copy.wait()


def gather_tiles(piece, n):
    pieces = {0: piece}
    for mask in range(3, n, 2):
        pieces[mask] = lax.ppermute(piece, "tile", [(i, i ^ mask) for i in range(n)])
    if n > 1:
        for mask in list(pieces):
            pieces[mask ^ 1] = lax.ppermute(pieces[mask], "tile", [(i, i ^ 1) for i in range(n)])
    masks = sorted(pieces)
    return masks, [pieces[m] for m in masks]


def exchange(arrays, n):
    got = []
    for k in range(1, n):
        got.append(lax.ppermute(arrays[k - 1], "survey", survey_pairs(k, n)))
    return got


def exchange_across(array, n, n_tile):
    got = []
    for k in range(1, n):
        pairs = [(s * n_tile + t, d * n_tile + (t ^ 1)) for s, d in survey_pairs(k, n) for t in range(n_tile)]
        got.append(lax.ppermute(array, ("survey", "tile"), pairs))
    return got


def call(kernel, out_shape, n_in, **options):
    single = not isinstance(out_shape, list)
    options = {"out_specs": VMEM if single else [VMEM] * len(out_shape), "in_specs": [VMEM] * n_in, **options}
    return pl.pallas_call(kernel, out_shape=out_shape, compiler_params=PARAMS, **options)


def local(n_survey, n_tile, data, correlation_index, correlation_count, smoothing):
    rows_x, rows_y, samples = data.shape[1:]
    total, cap = rows_x * rows_y, correlation_index.shape[-1]
    assert cap <= rows_y and samples % rows_y == 0 and samples <= 256 and is_power(samples) and is_power(n_tile) and n_tile > 1
    others = n_survey - 1
    smoothing = smoothing.reshape(1, 3)
    packed = jax.ShapeDtypeStruct((rows_y, samples), data.dtype)
    field_shape = jax.ShapeDtypeStruct((3, rows_x, rows_y), f32)
    term_shape = jax.ShapeDtypeStruct((6, rows_x, rows_y), f32)
    lane_shape = jax.ShapeDtypeStruct((others, samples, rows_y), f32)
    mask_shape = jax.ShapeDtypeStruct((others, rows_x, rows_y), f32)
    energy_shape = jax.ShapeDtypeStruct((others, 8, rows_y), f32)
    basis_shape = jax.ShapeDtypeStruct((2 * samples, samples), bf16)
    slope_shape = jax.ShapeDtypeStruct((total, samples), f32)
    volume_shape = jax.ShapeDtypeStruct((total, samples), data.dtype)
    grid = pltpu.VMEM((6, rows_x * n_tile, rows_y), f32)

    *outgoing, data = call(
        functools.partial(pack_kernel, n_survey),
        [packed] * others + [jax.ShapeDtypeStruct(data.shape, data.dtype)],
        2,
        in_specs=[HBM] * 2,
        scratch_shapes=[pltpu.VMEM(correlation_index.shape, jnp.int32), pltpu.SemaphoreType.DMA((2,))],
    )(*[pltpu.with_memory_space_constraint(a, pltpu.HBM) for a in (correlation_index, data)])
    arrived = exchange(outgoing, n_survey)
    basis, own, moved, mask, energy, slope = call(
        functools.partial(prepare_kernel, n_survey),
        [basis_shape, lane_shape, lane_shape, mask_shape, energy_shape, slope_shape],
        3,
    )(correlation_index, correlation_count, data)
    terms = []
    for slots in (range(1, others), range(1)):
        if len(slots):
            terms = call(
                functools.partial(pair_first_kernel, slots), term_shape, 5 + len(slots) + len(terms)
            )(basis, own, moved, mask, energy, *[arrived[k] for k in slots], *terms)
            terms = [terms]
    terms = terms[0]
    masks, pieces = gather_tiles(terms, n_tile)
    fields, beside = call(
        functools.partial(solve_first_kernel, masks), [field_shape] * 2, 1 + n_tile, scratch_shapes=[grid]
    )(smoothing, *pieces)

    partner_fields = exchange_across(beside, n_survey, n_tile)
    own, moved, energy, partner, partner_moved = call(
        functools.partial(refresh_kernel, n_survey),
        [lane_shape, lane_shape, energy_shape, lane_shape, lane_shape],
        5 + others,
    )(fields, basis, own, moved, mask, *arrived)
    terms = call(functools.partial(pair_next_kernel, n_survey), term_shape, 6 + others)(
        own, moved, mask, energy, partner, partner_moved, *partner_fields
    )
    masks, pieces = gather_tiles(terms, n_tile)
    fields, volume = call(
        functools.partial(solve_last_kernel, masks),
        [field_shape, volume_shape],
        4 + n_tile,
        out_specs=[ANY, ANY],
        scratch_shapes=[
            grid,
            pltpu.VMEM((3, rows_x, rows_y), f32),
            pltpu.VMEM((total, samples), data.dtype),
            pltpu.SemaphoreType.DMA((rows_x + 1,)),
        ],
    )(smoothing, fields, data, slope, *pieces)
    return fields.reshape(1, 3, rows_x, rows_y), volume.reshape(1, rows_x, rows_y, samples)


def solution(mesh):
    placed = (
        P("survey", "tile", None, None),
        P(None, "tile", None, None),
        P(None, "tile", None),
        P(),
    )
    return jax.shard_map(
        functools.partial(local, mesh.shape["survey"], mesh.shape["tile"]),
        mesh=mesh,
        in_specs=placed,
        out_specs=(P("survey", None, "tile", None), P("survey", "tile", None, None)),
        check_vma=False,
    )
```
